256 devices in a mesh: rows: 16 (over y_lo, z), cols: 8 (over x, y_hi), dp: 2 (over core).
Axes of the slice: x: 4, y: 4 (y_hi: 2, y_lo: 2; y = y_hi * 2 + y_lo), z: 8, core: 2. Of those that a mesh axis runs over, the one named last changes fastest.
Arguments:
- features: bfloat16 [2, 32, 512, 2048], P('dp', None, 'rows', 'cols'), may hold values from -6 to 6
- shifts: int32 [2, 32, 2], P('dp'), may hold values from -16 to 16, as said below
- first_kernel: bfloat16 [9, 32, 32], replicated, may hold values from -0.375 to 0.375
- bottle_kernel: bfloat16 [9, 32, 32], replicated, may hold values from -0.375 to 0.375
- second_kernel: bfloat16 [9, 32, 32], replicated, may hold values from -0.375 to 0.375
- cotangent: bfloat16 [2, 32, 512, 2048], P('dp', None, 'rows', 'cols'), may hold values from -6 to 6
Outputs:
- prediction: bfloat16 [2, 32, 512, 2048], P('dp', None, 'rows', 'cols')
- first_grad: float32 [9, 32, 32], replicated
- second_grad: float32 [9, 32, 32], replicated
The draws below stay inside these ranges and needn't reach their ends.
Inputs may be any that keep to these rules, and one draw needn't show every extreme that they name: `shifts`: every image has one channel displaced by exactly 16 and another by exactly -16 along one direction.
All inputs are finite; a program needn't handle non-finite values.
Results may differ from the reference program's by a relative error of at most 0.0059.
Values may be sent and summed in bfloat16 or wider, within the bound.
A program may use at most 64 MiB of HBM per device.

```python
import math
import jax
import jax.numpy as jnp
from jax import lax

C = 32
MAXSHIFT = 16
POOL = 4
IMGS = 2
H = 512
W = 2048


def draw_shifts(key, part):
    base_key, high_key, low_key, comp_key = jax.random.split(key, 4)
    shift_table = jax.random.randint(base_key, (IMGS, C, 2), -MAXSHIFT, MAXSHIFT + 1)
    high_chan = jax.random.randint(high_key, (IMGS, 1, 1), 0, C)
    low_chan = (high_chan + jax.random.randint(low_key, (IMGS, 1, 1), 1, C)) % C
    component = jax.random.randint(comp_key, (IMGS, 1, 1), 0, 2)
    chan_pos = jnp.arange(C)[None, :, None]
    comp_pos = jnp.arange(2)[None, None, :]
    shift_table = jnp.where((chan_pos == high_chan) & (comp_pos == component), MAXSHIFT, shift_table)
    shift_table = jnp.where((chan_pos == low_chan) & (comp_pos == component), -MAXSHIFT, shift_table)
    return shift_table.astype(jnp.int32)


def levels(own_key, shape, cuts, smallest, largest):
    def one(dim, parts):
        steps = jax.random.uniform(jax.random.fold_in(jax.random.fold_in(own_key, 6), dim), (parts,), jnp.float32, smallest / len(cuts), largest / len(cuts))
        return jnp.repeat(jnp.exp(steps), shape[dim] // parts).reshape((-1,) + (1,) * (len(shape) - dim - 1))

    level = one(*cuts[0])
    for cut in cuts[1:]:
        level = level * one(*cut)
    return level


def centred(own_key, shape, scale, bound, cuts=(), dtype=jnp.bfloat16):
    drawn = jax.random.normal(own_key, shape, jnp.float32) * scale
    if len(cuts) > 0:
        drawn = levels(own_key, shape, cuts, -0.22, 0.18) * drawn
    return jnp.clip(drawn, min=-bound, max=bound).astype(dtype)


def setup_inputs(seed: int = 0) -> dict:
    key_of = jax.random.split(jax.random.key(seed), 7)
    return {
        "features": centred(key_of[0], (IMGS, C, H, W), 1.0, 6.0, ((0, 2), (2, 16), (3, 8))),
        "shifts": draw_shifts(jax.random.fold_in(key_of[6], 71), 0),
        "first_kernel": centred(key_of[2], (9, C, C), (9 * C) ** -0.5, 0.375),
        "bottle_kernel": centred(key_of[3], (9, C, C), (9 * C) ** -0.5, 0.375),
        "second_kernel": centred(key_of[4], (9, C, C), (9 * C) ** -0.5, 0.375),
        "cotangent": centred(key_of[5], (IMGS, C, H, W), 1.0, 6.0, ((0, 2), (2, 16), (3, 8))),
    }


def stored(values):
    return lax.optimization_barrier(values.astype(jnp.bfloat16))

def pad_spatial(values, margin):
    return jnp.pad(values, ((0, 0), (margin, margin), (margin, margin)))

def convolve_one(values, kernel, transpose):
    height = values.shape[1]
    span = values.shape[2]
    padded = pad_spatial(values.astype(jnp.float32), 1)
    weights = kernel.astype(jnp.float32)
    result = jnp.zeros((weights.shape[1], height, span), jnp.float32)
    for tap_index in range(9):
        row_off = tap_index // 3 - 1
        col_off = tap_index % 3 - 1
        if transpose:
            window = padded[:, 1 - row_off:1 - row_off + height, 1 - col_off:1 - col_off + span]
            result = result + jnp.einsum('oi,ohw->ihw', weights[tap_index], window)
        else:
            window = padded[:, 1 + row_off:1 + row_off + height, 1 + col_off:1 + col_off + span]
            result = result + jnp.einsum('oi,ihw->ohw', weights[tap_index], window)
    return result

def convolve_all(values, kernel, transpose):
    return lax.map(lambda single: convolve_one(single, kernel, transpose), values)

def correlate_one(grad_out, values):
    height = values.shape[1]
    span = values.shape[2]
    padded = pad_spatial(values.astype(jnp.float32), 1)
    upper = grad_out.astype(jnp.float32)
    pieces = []
    for tap_index in range(9):
        row_off = tap_index // 3 - 1
        col_off = tap_index % 3 - 1
        window = padded[:, 1 + row_off:1 + row_off + height, 1 + col_off:1 + col_off + span]
        pieces.append(jnp.einsum('ohw,ihw->oi', upper, window))
    return jnp.stack(pieces)

def correlate(grad_out, values):
    return lax.optimization_barrier(jnp.sum(lax.map(lambda pair: correlate_one(pair[0], pair[1]), (grad_out, values)), axis=0))

def pool_sum(values):
    shape = values.shape
    return values.reshape(shape[0], shape[1], shape[2] // POOL, POOL, shape[3] // POOL, POOL).sum(axis=(3, 5))

def upsample(values):
    return jnp.repeat(jnp.repeat(values, POOL, axis=2), POOL, axis=3)

def warp_image(features, shifts):
    padded = jnp.pad(features, ((0, 0), (0, 0), (MAXSHIFT, MAXSHIFT), (MAXSHIFT, MAXSHIFT)))

    def single_plane(channel_plane, row_shift, col_shift):
        return lax.dynamic_slice(channel_plane, ((MAXSHIFT + row_shift).astype(jnp.int32), (MAXSHIFT + col_shift).astype(jnp.int32)), (H, W))
    return jax.vmap(jax.vmap(single_plane))(padded, shifts[..., 0], shifts[..., 1])

def reference(features, shifts, first_kernel, bottle_kernel, second_kernel, cotangent):
    warped = warp_image(features, shifts)
    first_pre = convolve_all(warped, first_kernel, False)
    first_act = stored(jax.nn.silu(first_pre))
    pooled = stored(pool_sum(first_act.astype(jnp.float32)) / (POOL * POOL))
    bottle = convolve_all(pooled, bottle_kernel, False)
    blended = stored(first_act.astype(jnp.float32) + upsample(bottle))
    prediction = convolve_all(blended, second_kernel, False).astype(jnp.bfloat16)
    blend_grad = stored(convolve_all(cotangent, second_kernel, True))
    coarse_grad = stored(pool_sum(blend_grad.astype(jnp.float32)))
    pooled_grad = convolve_all(coarse_grad, bottle_kernel, True)
    act_grad = blend_grad.astype(jnp.float32) + upsample(pooled_grad) / (POOL * POOL)
    sigma = jax.nn.sigmoid(first_pre)
    pre_grad = (act_grad * sigma * (1.0 + first_pre * (1.0 - sigma))).astype(jnp.bfloat16)
    factor = 1.0 / math.sqrt(IMGS * H * W)
    first_grad = correlate(pre_grad, warped) * factor
    second_grad = correlate(cotangent, blended) * factor
    return (prediction, first_grad, second_grad)
```

```python
import functools
import math

import jax
import jax.numpy as jnp
from jax import lax
from jax.experimental import pallas as pl
from jax.experimental.pallas import tpu as pltpu
from jax.sharding import PartitionSpec as P

C = 32
R = 32
S = 256
M = 16
B = 8
K = (B + 2) * 3 * C
F32 = jnp.float32
BF16 = jnp.bfloat16
MESH = pl.DeviceIdType.MESH


def lanes(shape):
    return lax.broadcasted_iota(jnp.int32, shape, len(shape) - 1)


def roll(x, amount):
    size = x.shape[1]
    amount = amount % size
    return x if amount == 0 else pltpu.roll(x, amount, 1)


def banded(taps):
    wide = jnp.concatenate([taps, jnp.zeros((C, 640), F32)], axis=1)
    return jnp.concatenate([roll(wide, 96 * r) for r in range(B)], axis=0)[:, :K].astype(BF16)


def edge_flags():
    row, col = lax.axis_index("rows"), lax.axis_index("cols")
    nrows, ncols = lax.axis_size("rows"), lax.axis_size("cols")
    return (
        jnp.where(row > 0, 1.0, 0.0),
        jnp.where(row < nrows - 1, 1.0, 0.0),
        jnp.where(col > 0, 1.0, 0.0),
        jnp.where(col < ncols - 1, 1.0, 0.0),
    )


def pack_kernel(feat_ref, cot_ref, g_ref, ct_ref, left_ref, right_ref, fs, cs):
    for c in range(C):
        for t in range(2):
            fs[t, pl.ds(c, R, stride=C), :] = feat_ref[0, c, :, t * 128 : t * 128 + 128].astype(F32)
            cs[t, pl.ds(c, R, stride=C), :] = cot_ref[0, c, :, t * 128 : t * 128 + 128].astype(F32)
    for t in range(2):
        cols = slice(t * 128, t * 128 + 128)
        g_ref[C : C + R * C, cols] = fs[t].astype(BF16)
        g_ref[0:C, cols] = cs[t, 0:C, :].astype(BF16)
        g_ref[C + R * C :, cols] = cs[t, (R - 1) * C :, :].astype(BF16)
        ct_ref[:, cols] = cs[t].astype(BF16)
    lane = lanes((128, 128))
    for h in range(2):
        low = jnp.zeros((128, 128), F32)
        high = jnp.zeros((128, 128), F32)
        for g in range(4):
            base = (16 * h + 4 * g) * C
            here = (lane >= 32 * g) & (lane < 32 * g + 32)
            part = jnp.where(lane < 17, fs[0, base : base + 128, :], roll(cs[0, base : base + 128, :], 17))
            low = jnp.where(here, roll(part, 32 * g), low)
            part = jnp.where(
                lane < 17, roll(fs[1, base : base + 128, :], 17), roll(cs[1, base : base + 128, :], 18)
            )
            high = jnp.where(here, roll(part, 32 * g), high)
        left_ref[h * 128 : h * 128 + 128, :] = low.astype(BF16)
        right_ref[h * 128 : h * 128 + 128, :] = high.astype(BF16)


def vmem(n):
    return [pl.BlockSpec(memory_space=pltpu.VMEM)] * n


def pack(features, cotangent):
    return pl.pallas_call(
        pack_kernel,
        out_shape=(
            jax.ShapeDtypeStruct(((R + 2) * C, S), BF16),
            jax.ShapeDtypeStruct((R * C, S), BF16),
            jax.ShapeDtypeStruct((256, 128), BF16),
            jax.ShapeDtypeStruct((256, 128), BF16),
        ),
        in_specs=vmem(2),
        out_specs=tuple(vmem(4)),
        scratch_shapes=[pltpu.VMEM((2, R * C, 128), F32)] * 2,
        name="pack",
    )(features, cotangent)


def neighbours():
    row, col = lax.axis_index("rows"), lax.axis_index("cols")
    nrows, ncols = lax.axis_size("rows"), lax.axis_size("cols")
    rows = (lax.rem(row + nrows - 1, nrows), row, lax.rem(row + 1, nrows))
    cols = (lax.rem(col + ncols - 1, ncols), col, lax.rem(col + 1, ncols))
    return lambda dr, dc: {"rows": rows[dr + 1], "cols": cols[dc + 1]}


def exchange(plan, inputs, shapes, collective_id, name):
    count = len(inputs)

    def kernel(*refs):
        ins, outs = refs[:count], refs[count : count + len(shapes)]
        send, recv = refs[count + len(shapes) :]
        device = neighbours()
        barrier = pltpu.get_barrier_semaphore()
        for dr, dc, *_ in plan:
            pl.semaphore_signal(barrier, inc=1, device_id=device(dr, dc), device_id_type=MESH)
        pl.semaphore_wait(barrier, len(plan))
        copies = []
        for n, (dr, dc, source, rows, target) in enumerate(plan):
            src = ins[source] if rows is None else ins[source].at[rows[0] : rows[1], :]
            copy = pltpu.make_async_remote_copy(
                src_ref=src,
                dst_ref=outs[target],
                send_sem=send.at[n],
                recv_sem=recv.at[n],
                device_id=device(dr, dc),
                device_id_type=MESH,
            )
            copy.start()
            copies.append(copy)
        for copy in copies:
            copy.wait()

    return pl.pallas_call(
        kernel,
        out_shape=tuple(jax.ShapeDtypeStruct(s, BF16) for s in shapes),
        in_specs=vmem(count),
        out_specs=tuple(vmem(len(shapes))),
        scratch_shapes=[pltpu.SemaphoreType.DMA((len(plan),)), pltpu.SemaphoreType.DMA((len(plan),))],
        compiler_params=pltpu.CompilerParams(collective_id=collective_id, has_side_effects=True),
        name=name,
    )(*inputs)


def exchange_inputs(g, left, right):
    plan = (
        (-1, 0, 0, (0, 18 * C), 1),
        (1, 0, 0, (16 * C, 34 * C), 0),
        (0, -1, 1, None, 3),
        (0, 1, 2, None, 2),
        (-1, -1, 1, (0, 160), 7),
        (1, -1, 1, (96, 256), 5),
        (-1, 1, 2, (0, 160), 6),
        (1, 1, 2, (96, 256), 4),
    )
    shapes = [(18 * C, S)] * 2 + [(256, 128)] * 2 + [(160, 128)] * 4
    return exchange(plan, (g, left, right), shapes, 0, "exchange_inputs")


def exchange_edges(up, down, left, right):
    plan = (
        (-1, 0, 0, None, 1),
        (1, 0, 1, None, 0),
        (0, -1, 2, None, 3),
        (0, 1, 3, None, 2),
        (-1, -1, 2, None, 7),
        (1, -1, 2, None, 5),
        (-1, 1, 3, None, 6),
        (1, 1, 3, None, 4),
    )
    shapes = [(160, 128)] * 2 + [(C, 128)] * 6
    return exchange(plan, (up, down, left, right), shapes, 1, "exchange_edges")


def with_edges(x, left, right):
    lane = lanes((x.shape[0], 128))
    back = pltpu.roll(x, 1, 1)
    ahead = pltpu.roll(x, S - 1, 1)
    back = jnp.concatenate([jnp.where(lane == 0, left, back[:, 0:128]), back[:, 128:256]], axis=1)
    ahead = jnp.concatenate([ahead[:, 0:128], jnp.where(lane == 127, right, ahead[:, 128:256])], axis=1)
    return back, x, ahead


def store_three(ref, first_row, versions):
    for b in range(3):
        value = versions[b].astype(BF16)
        for n in range(value.shape[0] // C):
            at = (first_row + n) * 96 + b * C
            ref[at : at + C, :] = value[n * C : n * C + C, :]


def first_kernel_body(
    shift_ref, g_ref, ct_ref, up_ref, down_ref, left_ref, right_ref, ul_ref, ur_ref, dl_ref, dr_ref, tap_ref,
    act_ref, slope_ref, bg_ref, pool_ref, coarse_ref, x3_ref, mu_ref, md_ref, el_ref, er_ref,
    fe, xf, c3,
):
    has_up, has_down, has_left, has_right = edge_flags()

    for t in range(2):
        cols = slice(t * 128, t * 128 + 128)
        fe[t + 1, 0 : 17 * C, :] = up_ref[0 : 17 * C, cols].astype(F32) * has_up
        fe[t + 1, 17 * C : 49 * C, :] = g_ref[C : 33 * C, cols].astype(F32)
        fe[t + 1, 49 * C :, :] = down_ref[C : 18 * C, cols].astype(F32) * has_down
    for side, (u, m, d), offset, flag in (
        (0, (ul_ref, left_ref, dl_ref), 111, has_left),
        (3, (ur_ref, right_ref, dr_ref), 0, has_right),
    ):
        above, below = flag * has_up, flag * has_down
        fe[side, 0:C, :] = roll(u[0:C, :].astype(F32), offset - 96) * above
        fe[side, 65 * C :, :] = roll(d[128:160, :].astype(F32), offset) * below
        for g in range(4):
            turn = offset - 32 * g
            at = (1 + 4 * g) * C
            fe[side, at : at + 128, :] = roll(u[32:160, :].astype(F32), turn) * above
            at = (49 + 4 * g) * C
            fe[side, at : at + 128, :] = roll(d[0:128, :].astype(F32), turn) * below
            for h in range(2):
                at = (17 + 16 * h + 4 * g) * C
                fe[side, at : at + 128, :] = roll(m[h * 128 : h * 128 + 128, :].astype(F32), turn) * flag

    for c in range(C):
        row_shift, col_shift = shift_ref[0, c, 0], shift_ref[0, c, 1]
        x = jnp.concatenate(
            [fe[t, pl.ds((M + row_shift) * C + c, R + 2, stride=C), :] for t in range(4)], axis=1
        )
        for b in range(3):
            y = pltpu.roll(x, 385 - b - col_shift, 1)
            for t in range(2):
                xf[t, pl.ds(b * C + c, R + 2, stride=96), :] = y[:, t * 128 : t * 128 + 128]
    lane = lanes((C, S))
    first_lane = jnp.where(lane == 0, has_left, 1.0)
    last_lane = jnp.where(lane == S - 1, has_right, 1.0)
    for row in range(R + 2):
        scale = has_up if row == 0 else has_down if row == R + 1 else None
        for b in range(3):
            at = row * 96 + b * C
            value = jnp.concatenate([xf[0, at : at + C, :], xf[1, at : at + C, :]], axis=1)
            if b != 1:
                value = value * (first_lane if b == 0 else last_lane)
            if scale is not None:
                value = value * scale
            x3_ref[at : at + C, :] = value.astype(BF16)

    for h in range(2):
        for g in range(4):
            base = 16 * h + 4 * g
            left = roll(left_ref[h * 128 : h * 128 + 128, :].astype(F32), -(32 * g + 17)) * has_left
            right = roll(right_ref[h * 128 : h * 128 + 128, :].astype(F32), 127 - (32 * g + 17)) * has_right
            x = ct_ref[base * C : base * C + 128, :].astype(F32)
            store_three(c3, base + 1, with_edges(x, left, right))
    left = roll(ul_ref[128:160, :].astype(F32), -(96 + 17)) * (has_left * has_up)
    right = roll(ur_ref[128:160, :].astype(F32), 127 - (96 + 17)) * (has_right * has_up)
    store_three(c3, 0, with_edges(up_ref[17 * C :, :].astype(F32) * has_up, left, right))
    left = roll(dl_ref[0:32, :].astype(F32), -17) * (has_left * has_down)
    right = roll(dr_ref[0:32, :].astype(F32), 127 - 17) * (has_right * has_down)
    store_three(c3, R + 1, with_edges(down_ref[0:C, :].astype(F32) * has_down, left, right))

    weights = banded(tap_ref[0])
    back_weights = banded(tap_ref[2])
    cell = 32 + lax.shift_right_logical(lax.broadcasted_iota(jnp.int32, (S, 128), 0), 2)
    gather = jnp.where(cell == lanes((S, 128)), 1.0, 0.0).astype(BF16)
    for k in range(R // B):
        rows = slice(k * B * C, (k + 1) * B * C)
        depth = slice(k * B * 96, k * B * 96 + K)
        pre = jnp.dot(weights, x3_ref[depth, :], preferred_element_type=F32)
        sigma = 1.0 / (1.0 + jnp.exp(-pre))
        act = (pre * sigma).astype(BF16)
        act_ref[rows, :] = act
        slope_ref[rows, :] = sigma * (1.0 + pre * (1.0 - sigma))
        bg = jnp.dot(back_weights, c3[depth, :], preferred_element_type=F32).astype(BF16)
        bg_ref[rows, :] = bg
        for value, ref, factor in ((act, pool_ref, 1.0 / 16.0), (bg, coarse_ref, 1.0)):
            sums = jnp.dot(value, gather, preferred_element_type=F32)
            for j in range(2):
                four = sums[j * 128 : j * 128 + 128]
                four = (four[0:32] + four[32:64]) + (four[64:96] + four[96:128])
                at = (2 * k + j) * C
                ref[at : at + C, :] = (four * factor).astype(BF16)

    mu_ref[0:32, :] = act_ref[0:32, 0:128]
    mu_ref[32:64, :] = act_ref[0:32, 128:256]
    mu_ref[64:128, :] = pool_ref[0:64, :]
    mu_ref[128:160, :] = coarse_ref[0:32, :]
    md_ref[0:32, :] = act_ref[31 * C :, 0:128]
    md_ref[32:64, :] = act_ref[31 * C :, 128:256]
    md_ref[64:128, :] = pool_ref[192:256, :]
    md_ref[128:160, :] = coarse_ref[224:256, :]
    lane = lanes((C, 128))
    low = jnp.zeros((C, 128), F32)
    high = jnp.zeros((C, 128), F32)
    for j in range(8):
        for v in range(4):
            at = (4 * j + v) * C
            t = 8 * j + v
            low = jnp.where(lane == t, roll(act_ref[at : at + C, 0:128].astype(F32), t), low)
            high = jnp.where(lane == t, roll(act_ref[at : at + C, 128:256].astype(F32), t - 127), high)
        t = 8 * j + 4
        two = (lane == t) | (lane == t + 1)
        value = pool_ref[j * C : j * C + C, :].astype(F32)
        low = jnp.where(two, roll(value, t - 32), low)
        high = jnp.where(two, roll(value, t - 94), high)
        t = 8 * j + 6
        value = coarse_ref[j * C : j * C + C, :].astype(F32)
        low = jnp.where(lane == t, roll(value, t - 32), low)
        high = jnp.where(lane == t, roll(value, t - 95), high)
    el_ref[...] = low.astype(BF16)
    er_ref[...] = high.astype(BF16)


def first_half(shifts, g, ct, halos, taps):
    shapes = (
        ((R * C, S), BF16),
        ((R * C, S), F32),
        ((R * C, S), BF16),
        ((256, 128), BF16),
        ((256, 128), BF16),
        (((R + 2) * 96, S), BF16),
        ((160, 128), BF16),
        ((160, 128), BF16),
        ((C, 128), BF16),
        ((C, 128), BF16),
    )
    return pl.pallas_call(
        first_kernel_body,
        out_shape=tuple(jax.ShapeDtypeStruct(s, d) for s, d in shapes),
        in_specs=[pl.BlockSpec(memory_space=pltpu.SMEM)] + vmem(11),
        out_specs=tuple(vmem(10)),
        scratch_shapes=[
            pltpu.VMEM((4, 66 * C, 128), F32),
            pltpu.VMEM((2, (R + 2) * 96, 128), F32),
            pltpu.VMEM(((R + 2) * 96, S), BF16),
        ],
        name="first_half",
    )(shifts, g, ct, *halos, taps)


def halves(x):
    high = x.astype(BF16)
    low = (x - high.astype(F32)).astype(BF16)
    return jnp.concatenate([high, low], axis=1)


def spread(b):
    cell = lax.rem(lax.broadcasted_iota(jnp.int32, (256, S), 0), 128)
    want = 31 + lax.shift_right_logical(lanes((256, S)) + (b - 1 + 4), 2)
    return jnp.where(cell == want, 1.0, 0.0).astype(BF16)


def collected(total, factor):
    groups = []
    for m in range(4):
        groups.append(
            total[m * 96 : m * 96 + 288, 0:128] + total[(m + 4) * 96 : (m + 4) * 96 + 288, 128:256]
        )
    lane = lanes((72, 128))
    result = jnp.zeros((72, 128), F32)
    for q in range(4):
        part = slice(72 * q, 72 * q + 72)
        value = sum(roll(groups[m][part], 32 * (q - m)) for m in range(4))
        result = jnp.where((lane >= 32 * q) & (lane < 32 * q + 32), value, result)
    return result * factor


def contract(a, b):
    return lax.dot_general(a, b, (((1,), (1,)), ((), ())), preferred_element_type=F32)


def second_kernel_body(
    factor,
    act_ref, slope_ref, bg_ref, pool_ref, coarse_ref, x3_ref, ct_ref,
    mu_ref, md_ref, el_ref, er_ref, ul_ref, ur_ref, dl_ref, dr_ref, tap_ref,
    pred_ref, grad_ref,
    p3, b3, pg, pf, up0, up1, up2,
):
    has_up, has_down, has_left, has_right = edge_flags()
    lane = lanes((C, 128))
    left_tiles = [ul_ref] * 2 + [el_ref] * 8 + [dl_ref] * 2
    right_tiles = [ur_ref] * 2 + [er_ref] * 8 + [dr_ref] * 2

    def coarse_rows(width, centre):
        first_row = -width
        for row in range(-width, 8 + width):
            j = row % 8
            above = has_up if row < 0 else has_down if row >= 8 else 1.0
            t = 8 * j + (4 if width == 2 else 6)
            span = 2 if width == 2 else 1
            x = centre(row).astype(F32)
            left = roll(left_tiles[row + 2][...].astype(F32), 32 - span - t)
            right = roll(right_tiles[row + 2][...].astype(F32), 96 - t)
            x = jnp.where((lane >= 32 - span) & (lane < 32), left * has_left, x)
            x = jnp.where((lane >= 96) & (lane < 96 + span), right * has_right, x)
            if row < 0 or row >= 8:
                x = x * above
            for b in range(3):
                at = (row - first_row) * 96 + b * C
                p3[at : at + C, :] = roll(x, 1 - b).astype(BF16)

    def pooled_row(row):
        if row < 0:
            return mu_ref[64 + (row + 2) * C : 64 + (row + 3) * C, :]
        if row >= 8:
            return md_ref[64 + (row - 8) * C : 64 + (row - 7) * C, :]
        return pool_ref[row * C : row * C + C, :]

    def coarse_row(row):
        if row < 0:
            return mu_ref[128:160, :]
        if row >= 8:
            return md_ref[128:160, :]
        return coarse_ref[row * C : row * C + C, :]

    coarse_rows(2, pooled_row)
    weights = banded(tap_ref[3])
    bottle = jnp.concatenate(
        [
            jnp.dot(weights, p3[0:K, :], preferred_element_type=F32),
            jnp.dot(weights, p3[192 : 192 + K, :], preferred_element_type=F32)[6 * C :],
        ],
        axis=0,
    )
    parts = halves(bottle)
    for b, ref in enumerate((up0, up1, up2)):
        ref[...] = jnp.dot(parts, spread(b), preferred_element_type=F32)

    for row in range(-1, R + 1):
        if row < 0:
            x = jnp.concatenate([mu_ref[0:32, :], mu_ref[32:64, :]], axis=1).astype(F32)
            low, high, t = ul_ref, ur_ref, 59
        elif row == R:
            x = jnp.concatenate([md_ref[0:32, :], md_ref[32:64, :]], axis=1).astype(F32)
            low, high, t = dl_ref, dr_ref, 0
        else:
            x = act_ref[row * C : row * C + C, :].astype(F32)
            low, high, t = el_ref, er_ref, 8 * (row // 4) + row % 4
        at = ((row + 4) // 4) * C
        ups = [ref[at : at + C, :] for ref in (up0, up1, up2)]
        back, mid, ahead = with_edges(x, roll(low[...].astype(F32), -t), roll(high[...].astype(F32), 127 - t))
        wide = lanes((C, S))
        back = (back + ups[0]) * jnp.where(wide == 0, has_left, 1.0)
        mid = mid + ups[1]
        ahead = (ahead + ups[2]) * jnp.where(wide == S - 1, has_right, 1.0)
        if row < 0 or row == R:
            keep = has_up if row < 0 else has_down
            back, mid, ahead = back * keep, mid * keep, ahead * keep
        store_three(b3, row + 1, (back, mid, ahead))

    coarse_rows(1, coarse_row)
    weights = banded(tap_ref[4])
    grad = jnp.dot(weights, p3[0:K, :], preferred_element_type=F32)
    up1[0:256, :] = jnp.dot(halves(grad), spread(1), preferred_element_type=F32) * (1.0 / 16.0)
    for row in range(R):
        at = slice(row * C, row * C + C)
        cell = (row // 4) * C
        value = (bg_ref[at, :].astype(F32) + up1[cell : cell + C, :]) * slope_ref[at, :]
        pg[at, :] = value.astype(BF16)

    weights = banded(tap_ref[1])
    first = second = None
    for k in range(R // B):
        rows = slice(k * B * C, (k + 1) * B * C)
        depth = slice(k * B * 96, k * B * 96 + K)
        value = jnp.dot(weights, b3[depth, :], preferred_element_type=F32)
        pf[0, rows, :] = value[:, 0:128]
        pf[1, rows, :] = value[:, 128:256]
        one = contract(b3[depth, :], ct_ref[rows, :])
        two = contract(x3_ref[depth, :], pg[rows, :])
        second = one if second is None else second + one
        first = two if first is None else first + two
    for o in range(C):
        for t in range(2):
            pred_ref[0, o, :, t * 128 : t * 128 + 128] = pf[t, pl.ds(o, R, stride=C), :].astype(BF16)
    both = jnp.concatenate([collected(first, factor), collected(second, factor)], axis=0)
    pieces, height = grad_ref.shape[:2]
    for n in range(pieces):
        grad_ref[n] = both[n * height : (n + 1) * height, :]


def second_half(factor, pieces, first, ct, edges, taps):
    act, slope, bg, pool, coarse, x3 = first
    return pl.pallas_call(
        functools.partial(second_kernel_body, factor),
        out_shape=(
            jax.ShapeDtypeStruct((1, C, R, S), BF16),
            jax.ShapeDtypeStruct((pieces, 144 // pieces, 128), F32),
        ),
        in_specs=vmem(16),
        out_specs=tuple(vmem(2)),
        scratch_shapes=[
            pltpu.VMEM((12 * 96, 128), BF16),
            pltpu.VMEM(((R + 2) * 96, S), BF16),
            pltpu.VMEM((R * C, S), BF16),
            pltpu.VMEM((2, R * C, 128), F32),
            pltpu.VMEM((10 * C, S), F32),
            pltpu.VMEM((10 * C, S), F32),
            pltpu.VMEM((10 * C, S), F32),
        ],
        name="second_half",
    )(act, slope, bg, pool, coarse, x3, ct, *edges, taps)


def reduce_kernel(grad_ref, out_ref, held, mine, column, send_a, recv_a, send_b, recv_b, send_c, recv_c):
    row, col, img = lax.axis_index("rows"), lax.axis_index("cols"), lax.axis_index("dp")
    nrows, ncols, ndp = lax.axis_size("rows"), lax.axis_size("cols"), lax.axis_size("dp")
    pieces = ncols * ndp
    me = col * ndp + img

    def peer(d):
        other = lax.rem(me + d, pieces)
        return other, {"cols": other // ndp, "dp": lax.rem(other, ndp)}

    def in_column(d):
        return {"rows": lax.rem(row + d, nrows)}

    barrier = pltpu.get_barrier_semaphore()
    for d in range(1, pieces):
        pl.semaphore_signal(barrier, inc=1, device_id=peer(d)[1], device_id_type=MESH)
    for d in range(1, nrows):
        pl.semaphore_signal(barrier, inc=1, device_id=in_column(d), device_id_type=MESH)
    pl.semaphore_wait(barrier, pieces + nrows - 2)

    copies = []
    for d in range(1, pieces):
        other, device = peer(d)
        copies.append(
            pltpu.make_async_remote_copy(
                src_ref=grad_ref.at[other],
                dst_ref=held.at[d],
                send_sem=send_a.at[d],
                recv_sem=recv_a.at[d],
                device_id=device,
                device_id_type=MESH,
            )
        )
        copies[-1].start()
    total = grad_ref[me]
    for d in range(1, pieces):
        copies[d - 1].wait_recv()
        total = total + held[d]
    mine[...] = total
    column[row] = total
    for d in range(1, nrows):
        copies.append(
            pltpu.make_async_remote_copy(
                src_ref=mine,
                dst_ref=column.at[row],
                send_sem=send_b.at[d],
                recv_sem=recv_b.at[d],
                device_id=in_column(d),
                device_id_type=MESH,
            )
        )
        copies[-1].start()
    for d in range(1, nrows):
        copies[pieces - 2 + d].wait_recv()
    total = column[0]
    for n in range(1, nrows):
        total = total + column[n]
    out_ref[me] = total
    for d in range(1, pieces):
        copies.append(
            pltpu.make_async_remote_copy(
                src_ref=out_ref.at[me],
                dst_ref=out_ref.at[me],
                send_sem=send_c.at[d],
                recv_sem=recv_c.at[d],
                device_id=peer(d)[1],
                device_id_type=MESH,
            )
        )
        copies[-1].start()
    for d in range(1, pieces):
        copies[pieces + nrows - 3 + d].wait_recv()
    for copy in copies:
        copy.wait_send()


def reduce_all(grads):
    pieces, height = grads.shape[:2]
    nrows = lax.axis_size("rows")
    piece = pltpu.VMEM((height, 128), F32)
    return pl.pallas_call(
        reduce_kernel,
        out_shape=jax.ShapeDtypeStruct(grads.shape, F32),
        in_specs=vmem(1),
        out_specs=vmem(1)[0],
        scratch_shapes=[
            pltpu.VMEM((pieces, height, 128), F32),
            piece,
            pltpu.VMEM((nrows, height, 128), F32),
        ]
        + [pltpu.SemaphoreType.DMA((n,)) for n in (pieces, pieces, nrows, nrows, pieces, pieces)],
        compiler_params=pltpu.CompilerParams(collective_id=2, has_side_effects=True),
        name="reduce_all",
    )(grads)


def tap_rows(kernel, transpose):
    if transpose:
        kernel = kernel[::-1]
    taps = kernel.reshape(3, 3, C, C).transpose((3, 0, 1, 2) if transpose else (2, 0, 1, 3))
    return jnp.pad(taps.reshape(C, 9 * C), ((0, 0), (0, 384 - 9 * C)))


def shards(features, shifts, first_kernel, bottle_kernel, second_kernel, cotangent):
    nrows, ncols, ndp = lax.axis_size("rows"), lax.axis_size("cols"), lax.axis_size("dp")
    assert features.shape == (1, C, R, S)
    taps = jnp.stack(
        [
            tap_rows(first_kernel, False),
            tap_rows(second_kernel, False),
            tap_rows(second_kernel, True),
            tap_rows(bottle_kernel, False),
            tap_rows(bottle_kernel, True),
        ]
    ).astype(F32)
    g, ct, left, right = pack(features, cotangent)
    halos = exchange_inputs(g, left, right)
    *first, mu, md, el, er = first_half(shifts, g, ct, halos, taps)
    edges = exchange_edges(mu, md, el, er)
    factor = 1.0 / math.sqrt(ndp * nrows * R * ncols * S)
    prediction, grads = second_half(factor, ncols * ndp, first, ct, edges, taps)
    grads = reduce_all(grads).reshape(2, 72, 4, C).transpose(0, 2, 1, 3)
    grads = grads.reshape(2, 9, C, C).transpose(0, 1, 3, 2)
    return prediction, grads[0], grads[1]


def solution(mesh):
    placed = (
        P("dp", None, "rows", "cols"),
        P("dp", None, None),
        P(),
        P(),
        P(),
        P("dp", None, "rows", "cols"),
    )
    return jax.shard_map(
        shards,
        mesh=mesh,
        in_specs=placed,
        out_specs=(P("dp", None, "rows", "cols"), P(), P()),
        check_vma=False,
    )
```

```python
import functools
import math

import jax
import jax.numpy as jnp
from jax import lax
from jax.experimental import pallas as pl
from jax.experimental.pallas import tpu as pltpu
from jax.sharding import PartitionSpec as P

C = 32
R = 32
S = 256
M = 16
B = 8
K = (B + 2) * 3 * C
F32 = jnp.float32
BF16 = jnp.bfloat16
MESH = pl.DeviceIdType.MESH


def lanes(shape):
    return lax.broadcasted_iota(jnp.int32, shape, len(shape) - 1)


def roll(x, amount):
    size = x.shape[1]
    amount = amount % size
    return x if amount == 0 else pltpu.roll(x, amount, 1)


def banded(taps):
    wide = jnp.concatenate([taps, jnp.zeros((C, 1024 - 9 * C), F32)], axis=1)
    return jnp.concatenate([roll(wide, 96 * r) for r in range(B)], axis=0)[:, :K].astype(BF16)


def forward_taps(ref):
    return jnp.concatenate([ref[t].astype(F32) for t in range(9)], axis=1)


def backward_taps(ref):
    return jnp.concatenate([ref[8 - t].astype(F32) for t in range(9)], axis=0).T


def edge_flags():
    row, col = lax.axis_index("rows"), lax.axis_index("cols")
    nrows, ncols = lax.axis_size("rows"), lax.axis_size("cols")
    return (
        jnp.where(row > 0, 1.0, 0.0),
        jnp.where(row < nrows - 1, 1.0, 0.0),
        jnp.where(col > 0, 1.0, 0.0),
        jnp.where(col < ncols - 1, 1.0, 0.0),
    )


def neighbours():
    row, col = lax.axis_index("rows"), lax.axis_index("cols")
    nrows, ncols = lax.axis_size("rows"), lax.axis_size("cols")
    rows = (lax.rem(row + nrows - 1, nrows), row, lax.rem(row + 1, nrows))
    cols = (lax.rem(col + ncols - 1, ncols), col, lax.rem(col + 1, ncols))
    return lambda dr, dc: {"rows": rows[dr + 1], "cols": cols[dc + 1]}


def with_edges(x, left, right):
    lane = lanes((x.shape[0], 128))
    back = pltpu.roll(x, 1, 1)
    ahead = pltpu.roll(x, S - 1, 1)
    back = jnp.concatenate([jnp.where(lane == 0, left, back[:, 0:128]), back[:, 128:256]], axis=1)
    ahead = jnp.concatenate([ahead[:, 0:128], jnp.where(lane == 127, right, ahead[:, 128:256])], axis=1)
    return back, x, ahead


def store_three(ref, first_row, versions):
    for b in range(3):
        value = versions[b].astype(BF16)
        for n in range(value.shape[0] // C):
            at = (first_row + n) * 96 + b * C
            ref[at : at + C, :] = value[n * C : n * C + C, :]


def halves(x):
    high = x.astype(BF16)
    low = (x - high.astype(F32)).astype(BF16)
    return jnp.concatenate([high, low], axis=1)


def spread(b):
    cell = lax.rem(lax.broadcasted_iota(jnp.int32, (256, S), 0), 128)
    want = 31 + lax.shift_right_logical(lanes((256, S)) + (b - 1 + 4), 2)
    return jnp.where(cell == want, 1.0, 0.0).astype(BF16)


def contract(a, b):
    return lax.dot_general(a, b, (((1,), (1,)), ((), ())), preferred_element_type=F32)


def collected(total, factor):
    result = None
    for r in range(B):
        block = total[r * C : r * C + C, :]
        block = roll(jnp.concatenate([block, jnp.zeros((C, 1024 - K), F32)], axis=1), -96 * r)[:, 0:384]
        result = block if result is None else result + block
    return result * factor


def ring_plan(up, down, left, right, left_up=None, left_down=None, right_up=None, right_down=None):
    return (
        (1, 0, down, 0),
        (-1, 0, up, 1),
        (0, 1, right, 2),
        (0, -1, left, 3),
        (1, 1, right if right_down is None else right_down, 4),
        (1, -1, left if left_down is None else left_down, 5),
        (-1, 1, right if right_up is None else right_up, 6),
        (-1, -1, left if left_up is None else left_up, 7),
    )


def half(x, t):
    return x[:, t * 128 : t * 128 + 128]


def both_halves(ref, rows):
    return jnp.concatenate([ref[0, rows, :], ref[1, rows, :]], axis=1)


def main_kernel(
    factor,
    feat_ref, cot_ref, shift_hbm, k1_ref, kb_ref, k2_ref,
    pred_ref, grad_ref,
    shift_ref, fs, cs, ft, ct, sl, sr, cl, cr, fe, xf, x3, c3, w1, w2, w2t, wb, wbt,
    act, slope, bg, pool, coarse, mu, md, el, er, gl, gr, p3, b3, pg, pf, up0, up1, up2,
    r_cot_row, r_cot_tile, r_row, r_strip, r_corner, r_gc_row, r_gc_tile, r_m, r_e,
    shift_sem, send, recv,
):
    device = neighbours()
    barrier = pltpu.get_barrier_semaphore()
    plan = ring_plan(*[None] * 4)
    for dr, dc, _, _ in plan:
        pl.semaphore_signal(barrier, inc=1, device_id=device(dr, dc), device_id_type=MESH)
    shift_copy = pltpu.make_async_copy(shift_hbm, shift_ref, shift_sem)
    shift_copy.start()
    has_up, has_down, has_left, has_right = edge_flags()
    started = []

    def start(stage, plan, targets):
        copies = []
        for dr, dc, source, n in plan:
            copies.append(
                pltpu.make_async_remote_copy(
                    src_ref=source,
                    dst_ref=targets[n],
                    send_sem=send.at[stage, n],
                    recv_sem=recv.at[stage, n],
                    device_id=device(dr, dc),
                    device_id_type=MESH,
                )
            )
            copies[-1].start()
        started.extend(copies)
        return copies

    def arrived(copies):
        for copy in copies:
            copy.wait_recv()

    lane = lanes((C, 128))
    for c in range(C):
        for t in range(2):
            cs[t, pl.ds(c, R, stride=C), :] = cot_ref[0, c, :, t * 128 : t * 128 + 128].astype(F32)
    low = jnp.zeros((C, 128), F32)
    high = jnp.zeros((C, 128), F32)
    for r in range(R):
        at = slice(r * C, r * C + C)
        low = jnp.where(lane == r, roll(cs[0, at, :], r), low)
        high = jnp.where(lane == r, roll(cs[1, at, :], r - 127), high)
    cl[...] = low.astype(BF16)
    cr[...] = high.astype(BF16)
    for t in range(2):
        ct[:, t * 128 : t * 128 + 128] = cs[t].astype(BF16)
    for c in range(C):
        for t in range(2):
            fs[t, pl.ds(c, R, stride=C), :] = feat_ref[0, c, :, t * 128 : t * 128 + 128].astype(F32)
    for t in range(2):
        ft[:, t * 128 : t * 128 + 128] = fs[t].astype(BF16)
    for p in range(5):
        low = jnp.zeros((C, 128), F32)
        high = jnp.zeros((C, 128), F32)
        for g in range(7):
            r = 7 * p + g
            if r < R:
                at = slice(r * C, r * C + C)
                here = (lane >= 18 * g) & (lane < 18 * g + 17)
                low = jnp.where(here, roll(fs[0, at, :], 18 * g), low)
                high = jnp.where(here, roll(fs[1, at, :], 18 * g + 17), high)
        sl[p * C : p * C + C, :] = low.astype(BF16)
        sr[p * C : p * C + C, :] = high.astype(BF16)
    pl.semaphore_wait(barrier, len(plan))
    cot_copies = start(
        0,
        ring_plan(ct.at[0:C, :], ct.at[(R - 1) * C : R * C, :], cl, cr),
        [r_cot_row.at[0], r_cot_row.at[1]] + [r_cot_tile.at[n] for n in range(6)],
    )
    feat_copies = start(
        1,
        ring_plan(
            ft.at[0 : 17 * C, :],
            ft.at[15 * C : R * C, :],
            sl,
            sr,
            sl.at[0:96, :],
            sl.at[64:160, :],
            sr.at[0:96, :],
            sr.at[64:160, :],
        ),
        [r_row.at[0], r_row.at[1], r_strip.at[0], r_strip.at[1]] + [r_corner.at[n] for n in range(4)],
    )

    w2t[...] = banded(backward_taps(k2_ref))
    w1[...] = banded(forward_taps(k1_ref))
    wbt[...] = banded(backward_taps(kb_ref))
    wb[...] = banded(forward_taps(kb_ref))
    w2[...] = banded(forward_taps(k2_ref))
    fe[1, 17 * C : 49 * C, :] = fs[0]
    fe[2, 17 * C : 49 * C, :] = fs[1]
    cell = 32 + lax.shift_right_logical(lax.broadcasted_iota(jnp.int32, (S, 128), 0), 2)
    gather = jnp.where(cell == lanes((S, 128)), 1.0, 0.0).astype(BF16)

    def pooled(value, k, ref, scale):
        sums = jnp.dot(value, gather, preferred_element_type=F32)
        for j in range(2):
            four = sums[j * 128 : j * 128 + 128]
            four = (four[0:32] + four[32:64]) + (four[64:96] + four[96:128])
            at = (2 * k + j) * C
            ref[at : at + C, :] = (four * scale).astype(BF16)

    arrived(cot_copies)
    tiles = [r_cot_tile[n].astype(F32) for n in range(6)]
    for r in range(-1, R + 1):
        if r < 0:
            x = r_cot_row[0].astype(F32) * has_up
            a, b, t, keep = tiles[2], tiles[3], R - 1, has_up
        elif r == R:
            x = r_cot_row[1].astype(F32) * has_down
            a, b, t, keep = tiles[4], tiles[5], 0, has_down
        else:
            x = both_halves(cs, slice(r * C, r * C + C))
            a, b, t, keep = tiles[0], tiles[1], r, 1.0
        store_three(
            c3, r + 1, with_edges(x, roll(a, -t) * (has_left * keep), roll(b, 127 - t) * (has_right * keep))
        )
    for k in range(R // B):
        rows = slice(k * B * C, (k + 1) * B * C)
        depth = slice(k * B * 96, k * B * 96 + K)
        value = jnp.dot(w2t[...], c3[depth, :], preferred_element_type=F32).astype(BF16)
        bg[rows, :] = value
        pooled(value, k, coarse, 1.0)
    low = jnp.zeros((C, 128), F32)
    high = jnp.zeros((C, 128), F32)
    for j in range(8):
        value = coarse[j * C : j * C + C, :].astype(F32)
        low = jnp.where(lane == j, roll(value, j - 32), low)
        high = jnp.where(lane == j, roll(value, j - 95), high)
    gl[...] = low.astype(BF16)
    gr[...] = high.astype(BF16)
    coarse_copies = start(
        2,
        ring_plan(coarse.at[0:C, :], coarse.at[7 * C : 8 * C, :], gl, gr),
        [r_gc_row.at[0], r_gc_row.at[1]] + [r_gc_tile.at[n] for n in range(6)],
    )

    arrived(feat_copies)
    for t in range(2):
        cols = slice(t * 128, t * 128 + 128)
        fe[t + 1, 0 : 17 * C, :] = r_row[0, :, cols].astype(F32) * has_up
        fe[t + 1, 49 * C :, :] = r_row[1, :, cols].astype(F32) * has_down
    for side, mid, above, below, offset, flag in (
        (0, r_strip.at[0], r_corner.at[0], r_corner.at[2], 111, has_left),
        (3, r_strip.at[1], r_corner.at[1], r_corner.at[3], 0, has_right),
    ):
        for r in range(-17, R + 17):
            if r < 0:
                source, their, first, keep = above, r + R, 2, flag * has_up
            elif r >= R:
                source, their, first, keep = below, r - R, 0, flag * has_down
            else:
                source, their, first, keep = mid, r, 0, flag
            at = (their // 7 - first) * C
            value = source[at : at + C, :].astype(F32)
            fe[side, (r + 17) * C : (r + 18) * C, :] = roll(value, offset - 18 * (their % 7)) * keep

    shift_copy.wait()
    for c in range(C):
        row_shift, col_shift = shift_ref[0, c, 0], shift_ref[0, c, 1]
        x = jnp.concatenate(
            [fe[t, pl.ds((M + row_shift) * C + c, R + 2, stride=C), :] for t in range(4)], axis=1
        )
        for b in range(3):
            y = pltpu.roll(x, 385 - b - col_shift, 1)
            for t in range(2):
                xf[t, pl.ds(b * C + c, R + 2, stride=96), :] = y[:, t * 128 : t * 128 + 128]
    wide = lanes((C, S))
    first_lane = jnp.where(wide == 0, has_left, 1.0)
    last_lane = jnp.where(wide == S - 1, has_right, 1.0)
    for row in range(R + 2):
        scale = has_up if row == 0 else has_down if row == R + 1 else None
        for b in range(3):
            at = row * 96 + b * C
            value = both_halves(xf, slice(at, at + C))
            if b != 1:
                value = value * (first_lane if b == 0 else last_lane)
            if scale is not None:
                value = value * scale
            x3[at : at + C, :] = value.astype(BF16)

    for k in range(R // B):
        rows = slice(k * B * C, (k + 1) * B * C)
        depth = slice(k * B * 96, k * B * 96 + K)
        pre = jnp.dot(w1[...], x3[depth, :], preferred_element_type=F32)
        sigma = 1.0 / (1.0 + jnp.exp(-pre))
        value = (pre * sigma).astype(BF16)
        act[rows, :] = value
        slope[rows, :] = sigma * (1.0 + pre * (1.0 - sigma))
        pooled(value, k, pool, 1.0 / 16.0)
    mu[0:32, :] = act[0:32, 0:128]
    mu[32:64, :] = act[0:32, 128:256]
    mu[64:128, :] = pool[0:64, :]
    md[0:32, :] = act[31 * C :, 0:128]
    md[32:64, :] = act[31 * C :, 128:256]
    md[64:128, :] = pool[192:256, :]
    low = jnp.zeros((C, 128), F32)
    high = jnp.zeros((C, 128), F32)
    for j in range(8):
        for v in range(4):
            at = (4 * j + v) * C
            t = 8 * j + v
            low = jnp.where(lane == t, roll(act[at : at + C, 0:128].astype(F32), t), low)
            high = jnp.where(lane == t, roll(act[at : at + C, 128:256].astype(F32), t - 127), high)
        t = 8 * j + 4
        two = (lane == t) | (lane == t + 1)
        value = pool[j * C : j * C + C, :].astype(F32)
        low = jnp.where(two, roll(value, t - 32), low)
        high = jnp.where(two, roll(value, t - 94), high)
    el[...] = low.astype(BF16)
    er[...] = high.astype(BF16)
    edge_copies = start(
        3, ring_plan(mu, md, el, er), [r_m.at[0], r_m.at[1]] + [r_e.at[n] for n in range(6)]
    )

    def cells(width, centre, tile_refs, lane_of):
        left_tiles = [2] * 2 + [0] * 8 + [4] * 2
        for row in range(-width, 8 + width):
            n = left_tiles[row + 2]
            t = lane_of(row % 8)
            x = centre(row).astype(F32)
            left = roll(tile_refs[n].astype(F32), 32 - width - t)
            right = roll(tile_refs[n + 1].astype(F32), 96 - t)
            x = jnp.where((lane >= 32 - width) & (lane < 32), left * has_left, x)
            x = jnp.where((lane >= 96) & (lane < 96 + width), right * has_right, x)
            if row < 0 or row >= 8:
                x = x * (has_up if row < 0 else has_down)
            for b in range(3):
                at = (row + width) * 96 + b * C
                p3[at : at + C, :] = roll(x, 1 - b).astype(BF16)

    def coarse_row(row):
        if row < 0 or row >= 8:
            return r_gc_row[0 if row < 0 else 1]
        return coarse[row * C : row * C + C, :]

    def pooled_row(row):
        if row < 0:
            return r_m[0, 64 + (row + 2) * C : 64 + (row + 3) * C, :]
        if row >= 8:
            return r_m[1, 64 + (row - 8) * C : 64 + (row - 7) * C, :]
        return pool[row * C : row * C + C, :]

    arrived(coarse_copies)
    cells(1, coarse_row, r_gc_tile, lambda j: j)
    grad = jnp.dot(wbt[...], p3[0:K, :], preferred_element_type=F32)
    spread_mid = spread(1)
    up1[0:256, :] = jnp.dot(halves(grad), spread_mid, preferred_element_type=F32) * (1.0 / 16.0)
    for row in range(R):
        at = slice(row * C, row * C + C)
        cell_at = (row // 4) * C
        value = (bg[at, :].astype(F32) + up1[cell_at : cell_at + C, :]) * slope[at, :]
        pg[at, :] = value.astype(BF16)
    total = None
    for k in range(R // B):
        rows = slice(k * B * C, (k + 1) * B * C)
        depth = slice(k * B * 96, k * B * 96 + K)
        part = contract(pg[rows, :], x3[depth, :])
        total = part if total is None else total + part
    first = collected(total, factor)

    arrived(edge_copies)
    cells(2, pooled_row, r_e, lambda j: 8 * j + 4)
    bottle = jnp.concatenate(
        [
            jnp.dot(wb[...], p3[0:K, :], preferred_element_type=F32),
            jnp.dot(wb[...], p3[192 : 192 + K, :], preferred_element_type=F32)[6 * C :],
        ],
        axis=0,
    )
    parts = halves(bottle)
    for b, ref in enumerate((up0, up1, up2)):
        ref[...] = jnp.dot(parts, spread_mid if b == 1 else spread(b), preferred_element_type=F32)

    tiles = [r_e[n].astype(F32) for n in range(6)]
    for row in range(-1, R + 1):
        if row < 0:
            x = jnp.concatenate([r_m[0, 0:32, :], r_m[0, 32:64, :]], axis=1).astype(F32)
            low, high, t = tiles[2], tiles[3], 59
        elif row == R:
            x = jnp.concatenate([r_m[1, 0:32, :], r_m[1, 32:64, :]], axis=1).astype(F32)
            low, high, t = tiles[4], tiles[5], 0
        else:
            x = act[row * C : row * C + C, :].astype(F32)
            low, high, t = tiles[0], tiles[1], 8 * (row // 4) + row % 4
        at = ((row + 4) // 4) * C
        back, mid, ahead = with_edges(x, roll(low, -t), roll(high, 127 - t))
        back = (back + up0[at : at + C, :]) * first_lane
        mid = mid + up1[at : at + C, :]
        ahead = (ahead + up2[at : at + C, :]) * last_lane
        if row < 0 or row == R:
            keep = has_up if row < 0 else has_down
            back, mid, ahead = back * keep, mid * keep, ahead * keep
        store_three(b3, row + 1, (back, mid, ahead))

    total = None
    for k in range(R // B):
        rows = slice(k * B * C, (k + 1) * B * C)
        depth = slice(k * B * 96, k * B * 96 + K)
        part = contract(ct[rows, :], b3[depth, :])
        total = part if total is None else total + part
    second = collected(total, factor)
    both = jnp.concatenate([half(x, t) for t in range(3) for x in (first, second)], axis=0)
    pieces, height = grad_ref.shape[:2]
    for n in range(pieces):
        grad_ref[n] = both[n * height : (n + 1) * height, :]
    for k in range(R // B):
        rows = slice(k * B * C, (k + 1) * B * C)
        depth = slice(k * B * 96, k * B * 96 + K)
        value = jnp.dot(w2[...], b3[depth, :], preferred_element_type=F32)
        pf[0, rows, :] = value[:, 0:128]
        pf[1, rows, :] = value[:, 128:256]
    for o in range(C):
        for t in range(2):
            pred_ref[0, o, :, t * 128 : t * 128 + 128] = pf[t, pl.ds(o, R, stride=C), :].astype(BF16)
    for copy in started:
        copy.wait_send()


def vmem(n):
    return [pl.BlockSpec(memory_space=pltpu.VMEM)] * n


def main(factor, pieces, features, cotangent, shifts, k1, kb, k2):
    def f(*shape):
        return pltpu.VMEM(shape, F32)

    def h(*shape):
        return pltpu.VMEM(shape, BF16)

    scratch = [pltpu.SMEM((1, C, 2), jnp.int32)]
    scratch += [f(2, R * C, 128), f(2, R * C, 128), h(R * C, S), h(R * C, S)]
    scratch += [h(160, 128), h(160, 128), h(C, 128), h(C, 128)]
    scratch += [f(4, 66 * C, 128), f(2, (R + 2) * 96, 128)]
    scratch += [h((R + 2) * 96, S), h((R + 2) * 96, S)] + [h(B * C, K)] * 5
    scratch += [h(R * C, S), f(R * C, S), h(R * C, S), h(256, 128), h(256, 128)]
    scratch += [h(128, 128), h(128, 128)] + [h(C, 128)] * 4
    scratch += [h(12 * 96, 128), h((R + 2) * 96, S), h(R * C, S), f(2, R * C, 128)]
    scratch += [f(10 * C, S)] * 3
    scratch += [h(2, C, S), h(6, C, 128), h(2, 17 * C, S), h(2, 160, 128), h(4, 96, 128)]
    scratch += [h(2, C, 128), h(6, C, 128), h(2, 128, 128), h(6, C, 128)]
    scratch += [pltpu.SemaphoreType.DMA, pltpu.SemaphoreType.DMA((4, 8)), pltpu.SemaphoreType.DMA((4, 8))]
    specs = vmem(6)
    specs[2] = pl.BlockSpec(memory_space=pl.ANY)
    return pl.pallas_call(
        functools.partial(main_kernel, factor),
        out_shape=(
            jax.ShapeDtypeStruct((1, C, R, S), BF16),
            jax.ShapeDtypeStruct((pieces, 192 // pieces, 128), F32),
        ),
        in_specs=specs,
        out_specs=tuple(vmem(2)),
        scratch_shapes=scratch,
        compiler_params=pltpu.CompilerParams(collective_id=0, has_side_effects=True),
        name="main",
    )(features, cotangent, shifts, k1, kb, k2)


def reduce_kernel(grad_ref, first_ref, second_ref, held, mine, column, out_ref, send_a, recv_a, send_b, recv_b, send_c, recv_c):
    row, col, img = lax.axis_index("rows"), lax.axis_index("cols"), lax.axis_index("dp")
    nrows, ncols, ndp = lax.axis_size("rows"), lax.axis_size("cols"), lax.axis_size("dp")
    pieces = ncols * ndp
    me = col * ndp + img

    def peer(d):
        other = lax.rem(me + d, pieces)
        return other, {"cols": other // ndp, "dp": lax.rem(other, ndp)}

    def in_column(d):
        return {"rows": lax.rem(row + d, nrows)}

    barrier = pltpu.get_barrier_semaphore()
    for d in range(1, pieces):
        pl.semaphore_signal(barrier, inc=1, device_id=peer(d)[1], device_id_type=MESH)
    for d in range(1, nrows):
        pl.semaphore_signal(barrier, inc=1, device_id=in_column(d), device_id_type=MESH)
    pl.semaphore_wait(barrier, pieces + nrows - 2)

    copies = []
    for d in range(1, pieces):
        other, device = peer(d)
        copies.append(
            pltpu.make_async_remote_copy(
                src_ref=grad_ref.at[other],
                dst_ref=held.at[d],
                send_sem=send_a.at[d],
                recv_sem=recv_a.at[d],
                device_id=device,
                device_id_type=MESH,
            )
        )
        copies[-1].start()
    total = grad_ref[me]
    for d in range(1, pieces):
        copies[d - 1].wait_recv()
        total = total + held[d]
    mine[...] = total
    column[row] = total
    for d in range(1, nrows):
        copies.append(
            pltpu.make_async_remote_copy(
                src_ref=mine,
                dst_ref=column.at[row],
                send_sem=send_b.at[d],
                recv_sem=recv_b.at[d],
                device_id=in_column(d),
                device_id_type=MESH,
            )
        )
        copies[-1].start()
    for d in range(1, nrows):
        copies[pieces - 2 + d].wait_recv()
    total = column[0]
    for n in range(1, nrows):
        total = total + column[n]
    out_ref[me] = total
    for d in range(1, pieces):
        copies.append(
            pltpu.make_async_remote_copy(
                src_ref=out_ref.at[me],
                dst_ref=out_ref.at[me],
                send_sem=send_c.at[d],
                recv_sem=recv_c.at[d],
                device_id=peer(d)[1],
                device_id_type=MESH,
            )
        )
        copies[-1].start()
    for d in range(1, pieces):
        copies[pieces + nrows - 3 + d].wait_recv()
    whole = jnp.concatenate([out_ref[n] for n in range(pieces)], axis=0)
    for t in range(9):
        for n, ref in enumerate((first_ref, second_ref)):
            at = (t // 4) * 64 + n * C
            ref[t] = roll(whole[at : at + C, :], -32 * (t % 4))[:, 0:C]
    for copy in copies:
        copy.wait_send()


def reduce_all(grads):
    pieces, height = grads.shape[:2]
    nrows = lax.axis_size("rows")
    piece = pltpu.VMEM((height, 128), F32)
    return pl.pallas_call(
        reduce_kernel,
        out_shape=(jax.ShapeDtypeStruct((9, C, C), F32),) * 2,
        in_specs=vmem(1),
        out_specs=tuple(vmem(2)),
        scratch_shapes=[
            pltpu.VMEM((pieces, height, 128), F32),
            piece,
            pltpu.VMEM((nrows, height, 128), F32),
            pltpu.VMEM((pieces, height, 128), F32),
        ]
        + [pltpu.SemaphoreType.DMA((n,)) for n in (pieces, pieces, nrows, nrows, pieces, pieces)],
        compiler_params=pltpu.CompilerParams(collective_id=2, has_side_effects=True),
        name="reduce_all",
    )(grads)


def shards(features, shifts, first_kernel, bottle_kernel, second_kernel, cotangent):
    nrows, ncols, ndp = lax.axis_size("rows"), lax.axis_size("cols"), lax.axis_size("dp")
    assert features.shape == (1, C, R, S)
    factor = 1.0 / math.sqrt(ndp * nrows * R * ncols * S)
    prediction, grads = main(
        factor, ncols * ndp, features, cotangent, shifts, first_kernel, bottle_kernel, second_kernel
    )
    first, second = reduce_all(grads)
    return prediction, first, second


def solution(mesh):
    placed = (
        P("dp", None, "rows", "cols"),
        P("dp", None, None),
        P(),
        P(),
        P(),
        P("dp", None, "rows", "cols"),
    )
    return jax.shard_map(
        shards,
        mesh=mesh,
        in_specs=placed,
        out_specs=(P("dp", None, "rows", "cols"), P(), P()),
        check_vma=False,
    )
```

```python
import functools
import math

import jax
import jax.numpy as jnp
from jax import lax
from jax.experimental import pallas as pl
from jax.experimental.pallas import tpu as pltpu
from jax.sharding import PartitionSpec as P

C = 32
R = 32
S = 256
M = 16
B = 8
K = (B + 2) * 3 * C
F32 = jnp.float32
BF16 = jnp.bfloat16
MESH = pl.DeviceIdType.MESH


def lanes(shape):
    return lax.broadcasted_iota(jnp.int32, shape, len(shape) - 1)


def roll(x, amount):
    size = x.shape[1]
    amount = amount % size
    return x if amount == 0 else pltpu.roll(x, amount, 1)


def banded(taps):
    wide = jnp.concatenate([taps, jnp.zeros((C, 1024 - 9 * C), F32)], axis=1)
    return jnp.concatenate([roll(wide, 96 * r) for r in range(B)], axis=0)[:, :K].astype(BF16)


def forward_taps(ref):
    return jnp.concatenate([ref[t].astype(F32) for t in range(9)], axis=1)


def backward_taps(ref):
    return jnp.concatenate([ref[8 - t].astype(F32) for t in range(9)], axis=0).T


def edge_flags():
    row, col = lax.axis_index("rows"), lax.axis_index("cols")
    nrows, ncols = lax.axis_size("rows"), lax.axis_size("cols")
    return (
        jnp.where(row > 0, 1.0, 0.0),
        jnp.where(row < nrows - 1, 1.0, 0.0),
        jnp.where(col > 0, 1.0, 0.0),
        jnp.where(col < ncols - 1, 1.0, 0.0),
    )


def neighbours():
    row, col = lax.axis_index("rows"), lax.axis_index("cols")
    nrows, ncols = lax.axis_size("rows"), lax.axis_size("cols")
    rows = (lax.rem(row + nrows - 1, nrows), row, lax.rem(row + 1, nrows))
    cols = (lax.rem(col + ncols - 1, ncols), col, lax.rem(col + 1, ncols))
    return lambda dr, dc: {"rows": rows[dr + 1], "cols": cols[dc + 1]}


def with_edges(x, left, right):
    lane = lanes((x.shape[0], 128))
    back = pltpu.roll(x, 1, 1)
    ahead = pltpu.roll(x, S - 1, 1)
    back = jnp.concatenate([jnp.where(lane == 0, left, back[:, 0:128]), back[:, 128:256]], axis=1)
    ahead = jnp.concatenate([ahead[:, 0:128], jnp.where(lane == 127, right, ahead[:, 128:256])], axis=1)
    return back, x, ahead


def store_three(ref, first_row, versions):
    for b in range(3):
        value = versions[b].astype(BF16)
        for n in range(value.shape[0] // C):
            at = (first_row + n) * 96 + b * C
            ref[at : at + C, :] = value[n * C : n * C + C, :]


def halves(x):
    high = x.astype(BF16)
    low = (x - high.astype(F32)).astype(BF16)
    return jnp.concatenate([high, low], axis=1)


def spread(b):
    cell = lax.rem(lax.broadcasted_iota(jnp.int32, (256, S), 0), 128)
    want = 31 + lax.shift_right_logical(lanes((256, S)) + (b - 1 + 4), 2)
    return jnp.where(cell == want, 1.0, 0.0).astype(BF16)


def contract(a, b):
    return lax.dot_general(a, b, (((1,), (1,)), ((), ())), preferred_element_type=F32)


def collected(total, factor):
    result = None
    for r in range(B):
        block = total[r * C : r * C + C, :]
        block = roll(jnp.concatenate([block, jnp.zeros((C, 1024 - K), F32)], axis=1), -96 * r)[:, 0:384]
        result = block if result is None else result + block
    return result * factor


def ring_plan(up, down, left, right, left_up=None, left_down=None, right_up=None, right_down=None):
    return (
        (1, 0, down, 0),
        (-1, 0, up, 1),
        (0, 1, right, 2),
        (0, -1, left, 3),
        (1, 1, right if right_down is None else right_down, 4),
        (1, -1, left if left_down is None else left_down, 5),
        (-1, 1, right if right_up is None else right_up, 6),
        (-1, -1, left if left_up is None else left_up, 7),
    )


def half(x, t):
    return x[:, t * 128 : t * 128 + 128]


def both_halves(ref, rows):
    return jnp.concatenate([ref[0, rows, :], ref[1, rows, :]], axis=1)


def main_kernel(
    factor,
    feat_ref, cot_ref, shift_ref, k1_ref, kb_ref, k2_ref,
    pred_ref, out_ref,
    fs, cs, ft, ct, sl, sr, cl, cr, fe, xf, x3, c3, w1, w2, w2t, wb, wbt,
    act, slope, bg, pool, coarse, mu, md, el, er, gl, gr, p3, b3, pg, pf, up0, up1, up2,
    r_cot_row, r_cot_tile, r_row, r_strip, r_corner, r_gc_row, r_gc_tile, r_m, r_e,
    grad_ref, held, mine, column,
    send, recv, send_a, recv_a, send_b, recv_b, send_c, recv_c,
):
    device = neighbours()
    my_row, col, img = lax.axis_index("rows"), lax.axis_index("cols"), lax.axis_index("dp")
    nrows, ncols, ndp = lax.axis_size("rows"), lax.axis_size("cols"), lax.axis_size("dp")
    pieces = ncols * ndp
    me = col * ndp + img

    def peer(d):
        other = lax.rem(me + d, pieces)
        return other, {"cols": other // ndp, "dp": lax.rem(other, ndp)}

    def in_column(d):
        return {"rows": lax.rem(my_row + d, nrows)}

    barrier = pltpu.get_barrier_semaphore()
    greeted = [device(dr, dc) for dr in (-1, 1) for dc in (-1, 1)]
    greeted += [in_column(d) for d in range(1, nrows)] + [peer(d)[1] for d in range(1, pieces)]
    for other in greeted:
        pl.semaphore_signal(barrier, inc=1, device_id=other, device_id_type=MESH)
    has_up, has_down, has_left, has_right = edge_flags()
    started = []

    def start(stage, plan, targets):
        copies = []
        for dr, dc, source, n in plan:
            copies.append(
                pltpu.make_async_remote_copy(
                    src_ref=source,
                    dst_ref=targets[n],
                    send_sem=send.at[stage, n],
                    recv_sem=recv.at[stage, n],
                    device_id=device(dr, dc),
                    device_id_type=MESH,
                )
            )
            copies[-1].start()
        started.extend(copies)
        return copies

    def arrived(copies):
        for copy in copies:
            copy.wait_recv()

    lane = lanes((C, 128))
    for c in range(C):
        for t in range(2):
            cs[t, pl.ds(c, R, stride=C), :] = cot_ref[0, c, :, t * 128 : t * 128 + 128].astype(F32)
    low = jnp.zeros((C, 128), F32)
    high = jnp.zeros((C, 128), F32)
    for r in range(R):
        at = slice(r * C, r * C + C)
        low = jnp.where(lane == r, roll(cs[0, at, :], r), low)
        high = jnp.where(lane == r, roll(cs[1, at, :], r - 127), high)
    cl[...] = low.astype(BF16)
    cr[...] = high.astype(BF16)
    for t in range(2):
        ct[:, t * 128 : t * 128 + 128] = cs[t].astype(BF16)
    for c in range(C):
        for t in range(2):
            fs[t, pl.ds(c, R, stride=C), :] = feat_ref[0, c, :, t * 128 : t * 128 + 128].astype(F32)
    for t in range(2):
        ft[:, t * 128 : t * 128 + 128] = fs[t].astype(BF16)
    for p in range(5):
        low = jnp.zeros((C, 128), F32)
        high = jnp.zeros((C, 128), F32)
        for g in range(7):
            r = 7 * p + g
            if r < R:
                at = slice(r * C, r * C + C)
                here = (lane >= 18 * g) & (lane < 18 * g + 17)
                low = jnp.where(here, roll(fs[0, at, :], 18 * g), low)
                high = jnp.where(here, roll(fs[1, at, :], 18 * g + 17), high)
        sl[p * C : p * C + C, :] = low.astype(BF16)
        sr[p * C : p * C + C, :] = high.astype(BF16)
    pl.semaphore_wait(barrier, len(greeted))
    cot_copies = start(
        0,
        ring_plan(ct.at[0:C, :], ct.at[(R - 1) * C : R * C, :], cl, cr),
        [r_cot_row.at[0], r_cot_row.at[1]] + [r_cot_tile.at[n] for n in range(6)],
    )
    feat_copies = start(
        1,
        ring_plan(
            ft.at[0 : 17 * C, :],
            ft.at[15 * C : R * C, :],
            sl,
            sr,
            sl.at[0:96, :],
            sl.at[64:160, :],
            sr.at[0:96, :],
            sr.at[64:160, :],
        ),
        [r_row.at[0], r_row.at[1], r_strip.at[0], r_strip.at[1]] + [r_corner.at[n] for n in range(4)],
    )

    w2t[...] = banded(backward_taps(k2_ref))
    w1[...] = banded(forward_taps(k1_ref))
    wbt[...] = banded(backward_taps(kb_ref))
    wb[...] = banded(forward_taps(kb_ref))
    w2[...] = banded(forward_taps(k2_ref))
    fe[1, 17 * C : 49 * C, :] = fs[0]
    fe[2, 17 * C : 49 * C, :] = fs[1]
    cell = 32 + lax.shift_right_logical(lax.broadcasted_iota(jnp.int32, (S, 128), 0), 2)
    gather = jnp.where(cell == lanes((S, 128)), 1.0, 0.0).astype(BF16)

    def pooled(value, k, ref, scale):
        sums = jnp.dot(value, gather, preferred_element_type=F32)
        for j in range(2):
            four = sums[j * 128 : j * 128 + 128]
            four = (four[0:32] + four[32:64]) + (four[64:96] + four[96:128])
            at = (2 * k + j) * C
            ref[at : at + C, :] = (four * scale).astype(BF16)

    arrived(cot_copies)
    tiles = [r_cot_tile[n].astype(F32) for n in range(6)]
    for r in range(-1, R + 1):
        if r < 0:
            x = r_cot_row[0].astype(F32) * has_up
            a, b, t, keep = tiles[2], tiles[3], R - 1, has_up
        elif r == R:
            x = r_cot_row[1].astype(F32) * has_down
            a, b, t, keep = tiles[4], tiles[5], 0, has_down
        else:
            x = both_halves(cs, slice(r * C, r * C + C))
            a, b, t, keep = tiles[0], tiles[1], r, 1.0
        store_three(
            c3, r + 1, with_edges(x, roll(a, -t) * (has_left * keep), roll(b, 127 - t) * (has_right * keep))
        )
    for k in range(R // B):
        rows = slice(k * B * C, (k + 1) * B * C)
        depth = slice(k * B * 96, k * B * 96 + K)
        value = jnp.dot(w2t[...], c3[depth, :], preferred_element_type=F32).astype(BF16)
        bg[rows, :] = value
        pooled(value, k, coarse, 1.0)
    low = jnp.zeros((C, 128), F32)
    high = jnp.zeros((C, 128), F32)
    for j in range(8):
        value = coarse[j * C : j * C + C, :].astype(F32)
        low = jnp.where(lane == j, roll(value, j - 32), low)
        high = jnp.where(lane == j, roll(value, j - 95), high)
    gl[...] = low.astype(BF16)
    gr[...] = high.astype(BF16)
    coarse_copies = start(
        2,
        ring_plan(coarse.at[0:C, :], coarse.at[7 * C : 8 * C, :], gl, gr),
        [r_gc_row.at[0], r_gc_row.at[1]] + [r_gc_tile.at[n] for n in range(6)],
    )

    arrived(feat_copies)
    for t in range(2):
        cols = slice(t * 128, t * 128 + 128)
        fe[t + 1, 0 : 17 * C, :] = r_row[0, :, cols].astype(F32) * has_up
        fe[t + 1, 49 * C :, :] = r_row[1, :, cols].astype(F32) * has_down
    for side, mid, above, below, offset, flag in (
        (0, r_strip.at[0], r_corner.at[0], r_corner.at[2], 111, has_left),
        (3, r_strip.at[1], r_corner.at[1], r_corner.at[3], 0, has_right),
    ):
        for r in range(-17, R + 17):
            if r < 0:
                source, their, first, keep = above, r + R, 2, flag * has_up
            elif r >= R:
                source, their, first, keep = below, r - R, 0, flag * has_down
            else:
                source, their, first, keep = mid, r, 0, flag
            at = (their // 7 - first) * C
            value = source[at : at + C, :].astype(F32)
            fe[side, (r + 17) * C : (r + 18) * C, :] = roll(value, offset - 18 * (their % 7)) * keep

    for c in range(C):
        row_shift, col_shift = shift_ref[0, 0, c], shift_ref[0, 1, c]
        x = jnp.concatenate(
            [fe[t, pl.ds((M + row_shift) * C + c, R + 2, stride=C), :] for t in range(4)], axis=1
        )
        for b in range(3):
            y = pltpu.roll(x, 385 - b - col_shift, 1)
            for t in range(2):
                xf[t, pl.ds(b * C + c, R + 2, stride=96), :] = y[:, t * 128 : t * 128 + 128]
    wide = lanes((C, S))
    first_lane = jnp.where(wide == 0, has_left, 1.0)
    last_lane = jnp.where(wide == S - 1, has_right, 1.0)
    for row in range(R + 2):
        scale = has_up if row == 0 else has_down if row == R + 1 else None
        for b in range(3):
            at = row * 96 + b * C
            value = both_halves(xf, slice(at, at + C))
            if b != 1:
                value = value * (first_lane if b == 0 else last_lane)
            if scale is not None:
                value = value * scale
            x3[at : at + C, :] = value.astype(BF16)

    for k in range(R // B):
        rows = slice(k * B * C, (k + 1) * B * C)
        depth = slice(k * B * 96, k * B * 96 + K)
        pre = jnp.dot(w1[...], x3[depth, :], preferred_element_type=F32)
        sigma = 1.0 / (1.0 + jnp.exp(-pre))
        value = (pre * sigma).astype(BF16)
        act[rows, :] = value
        slope[rows, :] = sigma * (1.0 + pre * (1.0 - sigma))
        pooled(value, k, pool, 1.0 / 16.0)
    mu[0:32, :] = act[0:32, 0:128]
    mu[32:64, :] = act[0:32, 128:256]
    mu[64:128, :] = pool[0:64, :]
    md[0:32, :] = act[31 * C :, 0:128]
    md[32:64, :] = act[31 * C :, 128:256]
    md[64:128, :] = pool[192:256, :]
    low = jnp.zeros((C, 128), F32)
    high = jnp.zeros((C, 128), F32)
    for j in range(8):
        for v in range(4):
            at = (4 * j + v) * C
            t = 8 * j + v
            low = jnp.where(lane == t, roll(act[at : at + C, 0:128].astype(F32), t), low)
            high = jnp.where(lane == t, roll(act[at : at + C, 128:256].astype(F32), t - 127), high)
        t = 8 * j + 4
        two = (lane == t) | (lane == t + 1)
        value = pool[j * C : j * C + C, :].astype(F32)
        low = jnp.where(two, roll(value, t - 32), low)
        high = jnp.where(two, roll(value, t - 94), high)
    el[...] = low.astype(BF16)
    er[...] = high.astype(BF16)
    edge_copies = start(
        3, ring_plan(mu, md, el, er), [r_m.at[0], r_m.at[1]] + [r_e.at[n] for n in range(6)]
    )

    def cells(width, centre, tile_refs, lane_of):
        left_tiles = [2] * 2 + [0] * 8 + [4] * 2
        for row in range(-width, 8 + width):
            n = left_tiles[row + 2]
            t = lane_of(row % 8)
            x = centre(row).astype(F32)
            left = roll(tile_refs[n].astype(F32), 32 - width - t)
            right = roll(tile_refs[n + 1].astype(F32), 96 - t)
            x = jnp.where((lane >= 32 - width) & (lane < 32), left * has_left, x)
            x = jnp.where((lane >= 96) & (lane < 96 + width), right * has_right, x)
            if row < 0 or row >= 8:
                x = x * (has_up if row < 0 else has_down)
            for b in range(3):
                at = (row + width) * 96 + b * C
                p3[at : at + C, :] = roll(x, 1 - b).astype(BF16)

    def coarse_row(row):
        if row < 0 or row >= 8:
            return r_gc_row[0 if row < 0 else 1]
        return coarse[row * C : row * C + C, :]

    def pooled_row(row):
        if row < 0:
            return r_m[0, 64 + (row + 2) * C : 64 + (row + 3) * C, :]
        if row >= 8:
            return r_m[1, 64 + (row - 8) * C : 64 + (row - 7) * C, :]
        return pool[row * C : row * C + C, :]

    arrived(coarse_copies)
    cells(1, coarse_row, r_gc_tile, lambda j: j)
    grad = jnp.dot(wbt[...], p3[0:K, :], preferred_element_type=F32)
    spread_mid = spread(1)
    up1[0:256, :] = jnp.dot(halves(grad), spread_mid, preferred_element_type=F32) * (1.0 / 16.0)
    for row in range(R):
        at = slice(row * C, row * C + C)
        cell_at = (row // 4) * C
        value = (bg[at, :].astype(F32) + up1[cell_at : cell_at + C, :]) * slope[at, :]
        pg[at, :] = value.astype(BF16)
    total = None
    for k in range(R // B):
        rows = slice(k * B * C, (k + 1) * B * C)
        depth = slice(k * B * 96, k * B * 96 + K)
        part = contract(pg[rows, :], x3[depth, :])
        total = part if total is None else total + part
    first = collected(total, factor)

    arrived(edge_copies)
    cells(2, pooled_row, r_e, lambda j: 8 * j + 4)
    bottle = jnp.concatenate(
        [
            jnp.dot(wb[...], p3[0:K, :], preferred_element_type=F32),
            jnp.dot(wb[...], p3[192 : 192 + K, :], preferred_element_type=F32)[6 * C :],
        ],
        axis=0,
    )
    parts = halves(bottle)
    for b, ref in enumerate((up0, up1, up2)):
        ref[...] = jnp.dot(parts, spread_mid if b == 1 else spread(b), preferred_element_type=F32)

    tiles = [r_e[n].astype(F32) for n in range(6)]
    for row in range(-1, R + 1):
        if row < 0:
            x = jnp.concatenate([r_m[0, 0:32, :], r_m[0, 32:64, :]], axis=1).astype(F32)
            low, high, t = tiles[2], tiles[3], 59
        elif row == R:
            x = jnp.concatenate([r_m[1, 0:32, :], r_m[1, 32:64, :]], axis=1).astype(F32)
            low, high, t = tiles[4], tiles[5], 0
        else:
            x = act[row * C : row * C + C, :].astype(F32)
            low, high, t = tiles[0], tiles[1], 8 * (row // 4) + row % 4
        at = ((row + 4) // 4) * C
        back, mid, ahead = with_edges(x, roll(low, -t), roll(high, 127 - t))
        back = (back + up0[at : at + C, :]) * first_lane
        mid = mid + up1[at : at + C, :]
        ahead = (ahead + up2[at : at + C, :]) * last_lane
        if row < 0 or row == R:
            keep = has_up if row < 0 else has_down
            back, mid, ahead = back * keep, mid * keep, ahead * keep
        store_three(b3, row + 1, (back, mid, ahead))

    total = None
    for k in range(R // B):
        rows = slice(k * B * C, (k + 1) * B * C)
        depth = slice(k * B * 96, k * B * 96 + K)
        part = contract(ct[rows, :], b3[depth, :])
        total = part if total is None else total + part
    second = collected(total, factor)
    both = jnp.concatenate([half(x, t) for t in range(3) for x in (first, second)], axis=0)
    height = grad_ref.shape[1]
    for n in range(pieces):
        grad_ref[n] = both[n * height : (n + 1) * height, :]

    def send_to(device_id, source, target, send_sem, recv_sem):
        copy = pltpu.make_async_remote_copy(
            src_ref=source,
            dst_ref=target,
            send_sem=send_sem,
            recv_sem=recv_sem,
            device_id=device_id,
            device_id_type=MESH,
        )
        copy.start()
        started.append(copy)
        return copy

    copies = []
    for d in range(1, pieces):
        other, device_id = peer(d)
        copies.append(send_to(device_id, grad_ref.at[other], held.at[d], send_a.at[d], recv_a.at[d]))
    for k in range(R // B):
        rows = slice(k * B * C, (k + 1) * B * C)
        depth = slice(k * B * 96, k * B * 96 + K)
        value = jnp.dot(w2[...], b3[depth, :], preferred_element_type=F32)
        pf[0, rows, :] = value[:, 0:128]
        pf[1, rows, :] = value[:, 128:256]
    arrived(copies)
    total = grad_ref[me]
    for d in range(1, pieces):
        total = total + held[d]
    mine[...] = total
    column[my_row] = total
    copies = []
    for d in range(1, nrows):
        copies.append(send_to(in_column(d), mine, column.at[my_row], send_b.at[d], recv_b.at[d]))
    for o in range(C):
        for t in range(2):
            pred_ref[0, o, :, t * 128 : t * 128 + 128] = pf[t, pl.ds(o, R, stride=C), :].astype(BF16)
    arrived(copies)
    total = column[0]
    for n in range(1, nrows):
        total = total + column[n]
    out_ref[me] = total
    copies = []
    for d in range(1, pieces):
        copies.append(send_to(peer(d)[1], out_ref.at[me], out_ref.at[me], send_c.at[d], recv_c.at[d]))
    arrived(copies)
    for copy in started:
        copy.wait_send()


def vmem(n):
    return [pl.BlockSpec(memory_space=pltpu.VMEM)] * n


def main(factor, pieces, features, cotangent, shifts, k1, kb, k2):
    def f(*shape):
        return pltpu.VMEM(shape, F32)

    def h(*shape):
        return pltpu.VMEM(shape, BF16)

    height, nrows = 192 // pieces, lax.axis_size("rows")
    scratch = [f(2, R * C, 128), f(2, R * C, 128), h(R * C, S), h(R * C, S)]
    scratch += [h(160, 128), h(160, 128), h(C, 128), h(C, 128)]
    scratch += [f(4, 66 * C, 128), f(2, (R + 2) * 96, 128)]
    scratch += [h((R + 2) * 96, S), h((R + 2) * 96, S)] + [h(B * C, K)] * 5
    scratch += [h(R * C, S), f(R * C, S), h(R * C, S), h(256, 128), h(256, 128)]
    scratch += [h(128, 128), h(128, 128)] + [h(C, 128)] * 4
    scratch += [h(12 * 96, 128), h((R + 2) * 96, S), h(R * C, S), f(2, R * C, 128)]
    scratch += [f(10 * C, S)] * 3
    scratch += [h(2, C, S), h(6, C, 128), h(2, 17 * C, S), h(2, 160, 128), h(4, 96, 128)]
    scratch += [h(2, C, 128), h(6, C, 128), h(2, 128, 128), h(6, C, 128)]
    scratch += [f(pieces, height, 128), f(pieces, height, 128), f(height, 128), f(nrows, height, 128)]
    scratch += [pltpu.SemaphoreType.DMA((4, 8)), pltpu.SemaphoreType.DMA((4, 8))]
    scratch += [pltpu.SemaphoreType.DMA((n,)) for n in (pieces, pieces, nrows, nrows, pieces, pieces)]
    specs = vmem(6)
    specs[2] = pl.BlockSpec(memory_space=pltpu.SMEM)
    return pl.pallas_call(
        functools.partial(main_kernel, factor),
        out_shape=(
            jax.ShapeDtypeStruct((1, C, R, S), BF16),
            jax.ShapeDtypeStruct((pieces, 192 // pieces, 128), F32),
        ),
        in_specs=specs,
        out_specs=tuple(vmem(2)),
        scratch_shapes=scratch,
        compiler_params=pltpu.CompilerParams(collective_id=0, has_side_effects=True),
        name="main",
    )(features, cotangent, shifts, k1, kb, k2)


def finish_kernel(pred_ref, sums_ref, out_ref, first_ref, second_ref):
    out_ref[...] = pred_ref[...]
    whole = jnp.concatenate([sums_ref[n] for n in range(sums_ref.shape[0])], axis=0)
    for t in range(9):
        for n, ref in enumerate((first_ref, second_ref)):
            at = (t // 4) * 64 + n * C
            ref[t] = roll(whole[at : at + C, :], -32 * (t % 4))[:, 0:C]


def finish(prediction, sums):
    return pl.pallas_call(
        finish_kernel,
        out_shape=(jax.ShapeDtypeStruct(prediction.shape, BF16),)
        + (jax.ShapeDtypeStruct((9, C, C), F32),) * 2,
        in_specs=vmem(2),
        out_specs=tuple(vmem(3)),
        name="finish",
    )(prediction, sums)


def shards(features, shifts, first_kernel, bottle_kernel, second_kernel, cotangent):
    nrows, ncols, ndp = lax.axis_size("rows"), lax.axis_size("cols"), lax.axis_size("dp")
    assert features.shape == (1, C, R, S)
    factor = 1.0 / math.sqrt(ndp * nrows * R * ncols * S)
    prediction, grads = main(
        factor, ncols * ndp, features, cotangent, shifts.transpose(0, 2, 1), first_kernel, bottle_kernel, second_kernel
    )
    return finish(prediction, grads)


def solution(mesh):
    placed = (
        P("dp", None, "rows", "cols"),
        P("dp", None, None),
        P(),
        P(),
        P(),
        P("dp", None, "rows", "cols"),
    )
    return jax.shard_map(
        shards,
        mesh=mesh,
        in_specs=placed,
        out_specs=(P("dp", None, "rows", "cols"), P(), P()),
        check_vma=False,
    )
```

```python
import functools
import math

import jax
import jax.numpy as jnp
from jax import lax
from jax.experimental import pallas as pl
from jax.experimental.pallas import tpu as pltpu
from jax.sharding import PartitionSpec as P

C = 32
R = 32
S = 256
M = 16
B = 8
K = (B + 2) * 3 * C
PITCH = C + 1
F32 = jnp.float32
BF16 = jnp.bfloat16
MESH = pl.DeviceIdType.MESH


def lanes(shape):
    return lax.broadcasted_iota(jnp.int32, shape, len(shape) - 1)


def roll(x, amount):
    size = x.shape[1]
    amount = amount % size
    return x if amount == 0 else pltpu.roll(x, amount, 1)


def banded(taps):
    wide = jnp.concatenate([taps, jnp.zeros((C, 1024 - 9 * C), F32)], axis=1)
    return jnp.concatenate([roll(wide, 96 * r) for r in range(B)], axis=0)[:, :K].astype(BF16)


def forward_taps(ref):
    return jnp.concatenate([ref[t].astype(F32) for t in range(9)], axis=1)


def backward_taps(ref):
    return jnp.concatenate([ref[8 - t].astype(F32) for t in range(9)], axis=0).T


def edge_flags():
    row, col = lax.axis_index("rows"), lax.axis_index("cols")
    nrows, ncols = lax.axis_size("rows"), lax.axis_size("cols")
    return (
        jnp.where(row > 0, 1.0, 0.0),
        jnp.where(row < nrows - 1, 1.0, 0.0),
        jnp.where(col > 0, 1.0, 0.0),
        jnp.where(col < ncols - 1, 1.0, 0.0),
    )


def neighbours():
    row, col = lax.axis_index("rows"), lax.axis_index("cols")
    nrows, ncols = lax.axis_size("rows"), lax.axis_size("cols")
    rows = (lax.rem(row + nrows - 1, nrows), row, lax.rem(row + 1, nrows))
    cols = (lax.rem(col + ncols - 1, ncols), col, lax.rem(col + 1, ncols))
    return lambda dr, dc: {"rows": rows[dr + 1], "cols": cols[dc + 1]}


def with_edges(x, left, right):
    lane = lanes((x.shape[0], 128))
    back = pltpu.roll(x, 1, 1)
    ahead = pltpu.roll(x, S - 1, 1)
    back = jnp.concatenate([jnp.where(lane == 0, left, back[:, 0:128]), back[:, 128:256]], axis=1)
    ahead = jnp.concatenate([ahead[:, 0:128], jnp.where(lane == 127, right, ahead[:, 128:256])], axis=1)
    return back, x, ahead


def store_three(ref, first_row, versions):
    for b in range(3):
        value = versions[b].astype(BF16)
        for n in range(value.shape[0] // C):
            at = (first_row + n) * 96 + b * C
            ref[at : at + C, :] = value[n * C : n * C + C, :]


def halves(x):
    high = x.astype(BF16)
    low = (x - high.astype(F32)).astype(BF16)
    return jnp.concatenate([high, low], axis=1)


def spread(b):
    cell = lax.rem(lax.broadcasted_iota(jnp.int32, (256, S), 0), 128)
    want = 31 + lax.shift_right_logical(lanes((256, S)) + (b - 1 + 4), 2)
    return jnp.where(cell == want, 1.0, 0.0).astype(BF16)


def contract(a, b):
    return lax.dot_general(a, b, (((1,), (1,)), ((), ())), preferred_element_type=F32)


def collected(total, factor):
    result = None
    for r in range(B):
        block = total[r * C : r * C + C, :]
        block = roll(jnp.concatenate([block, jnp.zeros((C, 1024 - K), F32)], axis=1), -96 * r)[:, 0:384]
        result = block if result is None else result + block
    return result * factor


def ring_plan(up, down, left, right, left_up=None, left_down=None, right_up=None, right_down=None):
    return (
        (1, 0, down, 0),
        (-1, 0, up, 1),
        (0, 1, right, 2),
        (0, -1, left, 3),
        (1, 1, right if right_down is None else right_down, 4),
        (1, -1, left if left_down is None else left_down, 5),
        (-1, 1, right if right_up is None else right_up, 6),
        (-1, -1, left if left_up is None else left_up, 7),
    )


def half(x, t):
    return x[:, t * 128 : t * 128 + 128]


def both_halves(ref, rows):
    return jnp.concatenate([ref[0, rows, :], ref[1, rows, :]], axis=1)


def main_kernel(
    factor,
    feat_ref, cot_ref, shift_ref, k1_ref, kb_ref, k2_ref,
    pred_ref, out_ref,
    ft, ct, sl, sr, cl, cr, fe, xf, x3, c3, w1, w2, w2t, wb, wbt,
    act, slope, bg, pool, coarse, mu, md, el, er, gl, gr, p3, b3, pg, pf, up0, up1, up2,
    r_cot_row, r_cot_tile, r_row, r_strip, r_corner, r_gc_row, r_gc_tile, r_m, r_e,
    grad_ref, held, mine, column,
    send, recv, send_a, recv_a, send_b, recv_b, send_c, recv_c,
):
    device = neighbours()
    my_row, col, img = lax.axis_index("rows"), lax.axis_index("cols"), lax.axis_index("dp")
    nrows, ncols, ndp = lax.axis_size("rows"), lax.axis_size("cols"), lax.axis_size("dp")
    pieces = ncols * ndp
    me = col * ndp + img

    def peer(d):
        other = lax.rem(me + d, pieces)
        return other, {"cols": other // ndp, "dp": lax.rem(other, ndp)}

    def in_column(d):
        return {"rows": lax.rem(my_row + d, nrows)}

    barrier = pltpu.get_barrier_semaphore()
    greeted = [device(dr, dc) for dr in (-1, 1) for dc in (-1, 1)]
    greeted += [in_column(d) for d in range(1, nrows)] + [peer(d)[1] for d in range(1, pieces)]
    for other in greeted:
        pl.semaphore_signal(barrier, inc=1, device_id=other, device_id_type=MESH)
    has_up, has_down, has_left, has_right = edge_flags()
    started = []

    def start(stage, plan, targets):
        copies = []
        for dr, dc, source, n in plan:
            copies.append(
                pltpu.make_async_remote_copy(
                    src_ref=source,
                    dst_ref=targets[n],
                    send_sem=send.at[stage, n],
                    recv_sem=recv.at[stage, n],
                    device_id=device(dr, dc),
                    device_id_type=MESH,
                )
            )
            copies[-1].start()
        started.extend(copies)
        return copies

    def arrived(copies):
        for copy in copies:
            copy.wait_recv()

    lane = lanes((C, 128))
    ct[...] = jnp.transpose(cot_ref[0], (1, 0, 2)).reshape(R * C, S)
    low = jnp.zeros((C, 128), BF16)
    high = jnp.zeros((C, 128), BF16)
    for r in range(R):
        at = slice(r * C, r * C + C)
        low = jnp.where(lane == r, roll(ct[at, 0:128], r), low)
        high = jnp.where(lane == r, roll(ct[at, 128:256], r - 127), high)
    cl[...] = low
    cr[...] = high
    ft[...] = jnp.transpose(feat_ref[0], (1, 0, 2)).reshape(R * C, S)
    for p in range(5):
        low = jnp.zeros((C, 128), BF16)
        high = jnp.zeros((C, 128), BF16)
        for g in range(7):
            r = 7 * p + g
            if r < R:
                at = slice(r * C, r * C + C)
                here = (lane >= 18 * g) & (lane < 18 * g + 17)
                low = jnp.where(here, roll(ft[at, 0:128], 18 * g), low)
                high = jnp.where(here, roll(ft[at, 128:256], 18 * g + 17), high)
        sl[p * C : p * C + C, :] = low
        sr[p * C : p * C + C, :] = high
    pl.semaphore_wait(barrier, len(greeted))
    cot_copies = start(
        0,
        ring_plan(ct.at[0:C, :], ct.at[(R - 1) * C : R * C, :], cl, cr),
        [r_cot_row.at[0], r_cot_row.at[1]] + [r_cot_tile.at[n] for n in range(6)],
    )
    feat_copies = start(
        1,
        ring_plan(
            ft.at[0 : 17 * C, :],
            ft.at[15 * C : R * C, :],
            sl,
            sr,
            sl.at[0:96, :],
            sl.at[64:160, :],
            sr.at[0:96, :],
            sr.at[64:160, :],
        ),
        [r_row.at[0], r_row.at[1], r_strip.at[0], r_strip.at[1]] + [r_corner.at[n] for n in range(4)],
    )

    w2t[...] = banded(backward_taps(k2_ref))
    w1[...] = banded(forward_taps(k1_ref))
    wbt[...] = banded(backward_taps(kb_ref))
    wb[...] = banded(forward_taps(kb_ref))
    w2[...] = banded(forward_taps(k2_ref))
    for r in range(R):
        for t in range(2):
            at = (r + 17) * PITCH
            fe[t + 1, at : at + C, :] = ft[r * C : r * C + C, t * 128 : t * 128 + 128].astype(F32)
    cell = 32 + lax.shift_right_logical(lax.broadcasted_iota(jnp.int32, (S, 128), 0), 2)
    gather = jnp.where(cell == lanes((S, 128)), 1.0, 0.0).astype(BF16)

    def pooled(value, k, ref, scale):
        sums = jnp.dot(value, gather, preferred_element_type=F32)
        for j in range(2):
            four = sums[j * 128 : j * 128 + 128]
            four = (four[0:32] + four[32:64]) + (four[64:96] + four[96:128])
            at = (2 * k + j) * C
            ref[at : at + C, :] = (four * scale).astype(BF16)

    arrived(cot_copies)
    tiles = [r_cot_tile[n] for n in range(6)]
    left_flag, right_flag = has_left.astype(BF16), has_right.astype(BF16)
    up_flag, down_flag = has_up.astype(BF16), has_down.astype(BF16)
    for r in range(-1, R + 1):
        if r < 0:
            x = r_cot_row[0] * up_flag
            a, b, t, keep = tiles[2], tiles[3], R - 1, up_flag
        elif r == R:
            x = r_cot_row[1] * down_flag
            a, b, t, keep = tiles[4], tiles[5], 0, down_flag
        else:
            x = ct[r * C : r * C + C, :]
            a, b, t, keep = tiles[0], tiles[1], r, None
        a, b = roll(a, -t) * left_flag, roll(b, 127 - t) * right_flag
        if keep is not None:
            a, b = a * keep, b * keep
        store_three(c3, r + 1, with_edges(x, a, b))
    for k in range(R // B):
        rows = slice(k * B * C, (k + 1) * B * C)
        depth = slice(k * B * 96, k * B * 96 + K)
        value = jnp.dot(w2t[...], c3[depth, :], preferred_element_type=F32).astype(BF16)
        bg[rows, :] = value
        pooled(value, k, coarse, 1.0)
    low = jnp.zeros((C, 128), BF16)
    high = jnp.zeros((C, 128), BF16)
    for j in range(8):
        value = coarse[j * C : j * C + C, :]
        low = jnp.where(lane == j, roll(value, j - 32), low)
        high = jnp.where(lane == j, roll(value, j - 95), high)
    gl[...] = low
    gr[...] = high
    coarse_copies = start(
        2,
        ring_plan(coarse.at[0:C, :], coarse.at[7 * C : 8 * C, :], gl, gr),
        [r_gc_row.at[0], r_gc_row.at[1]] + [r_gc_tile.at[n] for n in range(6)],
    )

    arrived(feat_copies)
    for t in range(2):
        cols = slice(t * 128, t * 128 + 128)
        for r in range(17):
            rows = slice(r * C, r * C + C)
            at = r * PITCH
            fe[t + 1, at : at + C, :] = r_row[0, rows, cols].astype(F32) * has_up
            at = (r + 49) * PITCH
            fe[t + 1, at : at + C, :] = r_row[1, rows, cols].astype(F32) * has_down
    for side, mid, above, below, offset, flag in (
        (0, r_strip.at[0], r_corner.at[0], r_corner.at[2], 111, has_left),
        (3, r_strip.at[1], r_corner.at[1], r_corner.at[3], 0, has_right),
    ):
        for r in range(-17, R + 17):
            if r < 0:
                source, their, first, keep = above, r + R, 2, flag * has_up
            elif r >= R:
                source, their, first, keep = below, r - R, 0, flag * has_down
            else:
                source, their, first, keep = mid, r, 0, flag
            at = (their // 7 - first) * C
            value = source[at : at + C, :].astype(F32)
            fe[side, (r + 17) * PITCH : (r + 17) * PITCH + C, :] = roll(value, offset - 18 * (their % 7)) * keep

    long_lane = lanes((R + 2, 128))
    for c in range(C):
        row_shift, col_shift = shift_ref[0, 0, c], shift_ref[0, 1, c]
        turn = lax.rem(128 - col_shift, 128)
        turned = [
            pltpu.roll(fe[t, pl.ds((M + row_shift) * PITCH + c, R + 2, stride=PITCH), :], turn, 1)
            for t in range(4)
        ]
        before = long_lane + col_shift < 0
        after = long_lane + col_shift >= 128
        rows = pl.ds(c, R + 2, stride=PITCH)
        for t in range(2):
            xf[t, rows, :] = jnp.where(before, turned[t], jnp.where(after, turned[t + 2], turned[t + 1]))
        xf[2, rows, :] = jnp.where(
            long_lane >= 64,
            jnp.where(after, turned[1], turned[0]),
            jnp.where(before, turned[2], turned[3]),
        )
    wide = lanes((C, S))
    first_lane = jnp.where(wide == 0, has_left, 1.0)
    last_lane = jnp.where(wide == S - 1, has_right, 1.0)
    edge_lane = jnp.where(lane >= 64, has_left, has_right)
    for row in range(R + 2):
        at = slice(row * PITCH, row * PITCH + C)
        x = both_halves(xf, at)
        edge = xf[2, at, :] * edge_lane
        if row == 0 or row == R + 1:
            keep = has_up if row == 0 else has_down
            x, edge = x * keep, edge * keep
        edge = edge.astype(BF16)
        store_three(x3, row, with_edges(x.astype(BF16), roll(edge, 1), roll(edge, 127)))

    for k in range(R // B):
        rows = slice(k * B * C, (k + 1) * B * C)
        depth = slice(k * B * 96, k * B * 96 + K)
        pre = jnp.dot(w1[...], x3[depth, :], preferred_element_type=F32)
        sigma = 1.0 / (1.0 + jnp.exp(-pre))
        value = (pre * sigma).astype(BF16)
        act[rows, :] = value
        slope[rows, :] = sigma * (1.0 + pre * (1.0 - sigma))
        pooled(value, k, pool, 1.0 / 16.0)
    mu[0:32, :] = act[0:32, 0:128]
    mu[32:64, :] = act[0:32, 128:256]
    mu[64:128, :] = pool[0:64, :]
    md[0:32, :] = act[31 * C :, 0:128]
    md[32:64, :] = act[31 * C :, 128:256]
    md[64:128, :] = pool[192:256, :]
    low = jnp.zeros((C, 128), BF16)
    high = jnp.zeros((C, 128), BF16)
    for j in range(8):
        for v in range(4):
            at = (4 * j + v) * C
            t = 8 * j + v
            low = jnp.where(lane == t, roll(act[at : at + C, 0:128], t), low)
            high = jnp.where(lane == t, roll(act[at : at + C, 128:256], t - 127), high)
        t = 8 * j + 4
        two = (lane == t) | (lane == t + 1)
        value = pool[j * C : j * C + C, :]
        low = jnp.where(two, roll(value, t - 32), low)
        high = jnp.where(two, roll(value, t - 94), high)
    el[...] = low
    er[...] = high
    edge_copies = start(
        3, ring_plan(mu, md, el, er), [r_m.at[0], r_m.at[1]] + [r_e.at[n] for n in range(6)]
    )

    def cells(width, centre, tile_refs, lane_of):
        left_tiles = [2] * 2 + [0] * 8 + [4] * 2
        for row in range(-width, 8 + width):
            n = left_tiles[row + 2]
            t = lane_of(row % 8)
            x = centre(row).astype(F32)
            left = roll(tile_refs[n].astype(F32), 32 - width - t)
            right = roll(tile_refs[n + 1].astype(F32), 96 - t)
            x = jnp.where((lane >= 32 - width) & (lane < 32), left * has_left, x)
            x = jnp.where((lane >= 96) & (lane < 96 + width), right * has_right, x)
            if row < 0 or row >= 8:
                x = x * (has_up if row < 0 else has_down)
            for b in range(3):
                at = (row + width) * 96 + b * C
                p3[at : at + C, :] = roll(x, 1 - b).astype(BF16)

    def coarse_row(row):
        if row < 0 or row >= 8:
            return r_gc_row[0 if row < 0 else 1]
        return coarse[row * C : row * C + C, :]

    def pooled_row(row):
        if row < 0:
            return r_m[0, 64 + (row + 2) * C : 64 + (row + 3) * C, :]
        if row >= 8:
            return r_m[1, 64 + (row - 8) * C : 64 + (row - 7) * C, :]
        return pool[row * C : row * C + C, :]

    arrived(coarse_copies)
    cells(1, coarse_row, r_gc_tile, lambda j: j)
    grad = jnp.dot(wbt[...], p3[0:K, :], preferred_element_type=F32)
    spread_mid = spread(1)
    up1[0:256, :] = jnp.dot(halves(grad), spread_mid, preferred_element_type=F32) * (1.0 / 16.0)
    for row in range(R):
        at = slice(row * C, row * C + C)
        cell_at = (row // 4) * C
        value = (bg[at, :].astype(F32) + up1[cell_at : cell_at + C, :]) * slope[at, :]
        pg[at, :] = value.astype(BF16)
    total = None
    for k in range(R // B):
        rows = slice(k * B * C, (k + 1) * B * C)
        depth = slice(k * B * 96, k * B * 96 + K)
        part = contract(pg[rows, :], x3[depth, :])
        total = part if total is None else total + part
    first = collected(total, factor)

    arrived(edge_copies)
    cells(2, pooled_row, r_e, lambda j: 8 * j + 4)
    bottle = jnp.concatenate(
        [
            jnp.dot(wb[...], p3[0:K, :], preferred_element_type=F32),
            jnp.dot(wb[...], p3[192 : 192 + K, :], preferred_element_type=F32)[6 * C :],
        ],
        axis=0,
    )
    parts = halves(bottle)
    for b, ref in enumerate((up0, up1, up2)):
        ref[...] = jnp.dot(parts, spread_mid if b == 1 else spread(b), preferred_element_type=F32)

    tiles = [r_e[n] for n in range(6)]
    for row in range(-1, R + 1):
        if row < 0:
            x = jnp.concatenate([r_m[0, 0:32, :], r_m[0, 32:64, :]], axis=1)
            low, high, t = tiles[2], tiles[3], 59
        elif row == R:
            x = jnp.concatenate([r_m[1, 0:32, :], r_m[1, 32:64, :]], axis=1)
            low, high, t = tiles[4], tiles[5], 0
        else:
            x = act[row * C : row * C + C, :]
            low, high, t = tiles[0], tiles[1], 8 * (row // 4) + row % 4
        at = ((row + 4) // 4) * C
        back, mid, ahead = with_edges(x, roll(low, -t), roll(high, 127 - t))
        back = (back.astype(F32) + up0[at : at + C, :]) * first_lane
        mid = mid.astype(F32) + up1[at : at + C, :]
        ahead = (ahead.astype(F32) + up2[at : at + C, :]) * last_lane
        if row < 0 or row == R:
            keep = has_up if row < 0 else has_down
            back, mid, ahead = back * keep, mid * keep, ahead * keep
        store_three(b3, row + 1, (back, mid, ahead))

    total = None
    for k in range(R // B):
        rows = slice(k * B * C, (k + 1) * B * C)
        depth = slice(k * B * 96, k * B * 96 + K)
        part = contract(ct[rows, :], b3[depth, :])
        total = part if total is None else total + part
    second = collected(total, factor)
    both = jnp.concatenate([half(x, t) for t in range(3) for x in (first, second)], axis=0)
    height = grad_ref.shape[1]
    for n in range(pieces):
        grad_ref[n] = both[n * height : (n + 1) * height, :]

    def send_to(device_id, source, target, send_sem, recv_sem):
        copy = pltpu.make_async_remote_copy(
            src_ref=source,
            dst_ref=target,
            send_sem=send_sem,
            recv_sem=recv_sem,
            device_id=device_id,
            device_id_type=MESH,
        )
        copy.start()
        started.append(copy)
        return copy

    copies = []
    for d in range(1, pieces):
        other, device_id = peer(d)
        copies.append(send_to(device_id, grad_ref.at[other], held.at[d], send_a.at[d], recv_a.at[d]))
    for k in range(R // B):
        rows = slice(k * B * C, (k + 1) * B * C)
        depth = slice(k * B * 96, k * B * 96 + K)
        pf[rows, :] = jnp.dot(w2[...], b3[depth, :], preferred_element_type=F32).astype(BF16)
    arrived(copies)
    total = grad_ref[me]
    for d in range(1, pieces):
        total = total + held[d]
    mine[...] = total
    column[my_row] = total
    copies = []
    for d in range(1, nrows):
        copies.append(send_to(in_column(d), mine, column.at[my_row], send_b.at[d], recv_b.at[d]))
    pred_ref[0] = jnp.transpose(pf[...].reshape(R, C, S), (1, 0, 2))
    arrived(copies)
    total = column[0]
    for n in range(1, nrows):
        total = total + column[n]
    out_ref[me] = total
    copies = []
    for d in range(1, pieces):
        copies.append(send_to(peer(d)[1], out_ref.at[me], out_ref.at[me], send_c.at[d], recv_c.at[d]))
    arrived(copies)
    for copy in started:
        copy.wait_send()


def vmem(n):
    return [pl.BlockSpec(memory_space=pltpu.VMEM)] * n


def main(factor, pieces, features, cotangent, shifts, k1, kb, k2):
    def f(*shape):
        return pltpu.VMEM(shape, F32)

    def h(*shape):
        return pltpu.VMEM(shape, BF16)

    height, nrows = 192 // pieces, lax.axis_size("rows")
    scratch = [h(R * C, S), h(R * C, S)]
    scratch += [h(160, 128), h(160, 128), h(C, 128), h(C, 128)]
    scratch += [f(4, 72 * PITCH, 128), f(3, (R + 8) * PITCH, 128)]
    scratch += [h((R + 2) * 96, S), h((R + 2) * 96, S)] + [h(B * C, K)] * 5
    scratch += [h(R * C, S), f(R * C, S), h(R * C, S), h(256, 128), h(256, 128)]
    scratch += [h(128, 128), h(128, 128)] + [h(C, 128)] * 4
    scratch += [h(12 * 96, 128), h((R + 2) * 96, S), h(R * C, S), h(R * C, S)]
    scratch += [f(10 * C, S)] * 3
    scratch += [h(2, C, S), h(6, C, 128), h(2, 17 * C, S), h(2, 160, 128), h(4, 96, 128)]
    scratch += [h(2, C, 128), h(6, C, 128), h(2, 128, 128), h(6, C, 128)]
    scratch += [f(pieces, height, 128), f(pieces, height, 128), f(height, 128), f(nrows, height, 128)]
    scratch += [pltpu.SemaphoreType.DMA((4, 8)), pltpu.SemaphoreType.DMA((4, 8))]
    scratch += [pltpu.SemaphoreType.DMA((n,)) for n in (pieces, pieces, nrows, nrows, pieces, pieces)]
    specs = vmem(6)
    specs[2] = pl.BlockSpec(memory_space=pltpu.SMEM)
    return pl.pallas_call(
        functools.partial(main_kernel, factor),
        out_shape=(
            jax.ShapeDtypeStruct((1, C, R, S), BF16),
            jax.ShapeDtypeStruct((pieces, 192 // pieces, 128), F32),
        ),
        in_specs=specs,
        out_specs=tuple(vmem(2)),
        scratch_shapes=scratch,
        compiler_params=pltpu.CompilerParams(collective_id=0, has_side_effects=True),
        name="main",
    )(features, cotangent, shifts, k1, kb, k2)


def finish_kernel(pred_ref, sums_ref, out_ref, first_ref, second_ref):
    out_ref[...] = pred_ref[...]
    whole = jnp.concatenate([sums_ref[n] for n in range(sums_ref.shape[0])], axis=0)
    for t in range(9):
        for n, ref in enumerate((first_ref, second_ref)):
            at = (t // 4) * 64 + n * C
            ref[t] = roll(whole[at : at + C, :], -32 * (t % 4))[:, 0:C]


def finish(prediction, sums):
    return pl.pallas_call(
        finish_kernel,
        out_shape=(jax.ShapeDtypeStruct(prediction.shape, BF16),)
        + (jax.ShapeDtypeStruct((9, C, C), F32),) * 2,
        in_specs=vmem(2),
        out_specs=tuple(vmem(3)),
        name="finish",
    )(prediction, sums)


def shards(features, shifts, first_kernel, bottle_kernel, second_kernel, cotangent):
    nrows, ncols, ndp = lax.axis_size("rows"), lax.axis_size("cols"), lax.axis_size("dp")
    assert features.shape == (1, C, R, S)
    factor = 1.0 / math.sqrt(ndp * nrows * R * ncols * S)
    prediction, grads = main(
        factor, ncols * ndp, features, cotangent, shifts.transpose(0, 2, 1), first_kernel, bottle_kernel, second_kernel
    )
    return finish(prediction, grads)


def solution(mesh):
    placed = (
        P("dp", None, "rows", "cols"),
        P("dp", None, None),
        P(),
        P(),
        P(),
        P("dp", None, "rows", "cols"),
    )
    return jax.shard_map(
        shards,
        mesh=mesh,
        in_specs=placed,
        out_specs=(P("dp", None, "rows", "cols"), P(), P()),
        check_vma=False,
    )
```

```python
import functools
import math

import jax
import jax.numpy as jnp
from jax import lax
from jax.experimental import pallas as pl
from jax.experimental.pallas import tpu as pltpu
from jax.sharding import PartitionSpec as P

C = 32
R = 32
S = 256
M = 16
B = 8
K = (B + 2) * 3 * C
PITCH = C + 1
F32 = jnp.float32
BF16 = jnp.bfloat16
MESH = pl.DeviceIdType.MESH


def lanes(shape):
    return lax.broadcasted_iota(jnp.int32, shape, len(shape) - 1)


def roll(x, amount):
    size = x.shape[1]
    amount = amount % size
    return x if amount == 0 else pltpu.roll(x, amount, 1)


def banded(taps):
    wide = jnp.concatenate([taps, jnp.zeros((C, 1024 - 9 * C), F32)], axis=1)
    return jnp.concatenate([roll(wide, 96 * r) for r in range(B)], axis=0)[:, :K].astype(BF16)


def forward_taps(ref):
    return jnp.concatenate([ref[t].astype(F32) for t in range(9)], axis=1)


def backward_taps(ref):
    return jnp.concatenate([ref[8 - t].astype(F32) for t in range(9)], axis=0).T


def edge_flags():
    row, col = lax.axis_index("rows"), lax.axis_index("cols")
    nrows, ncols = lax.axis_size("rows"), lax.axis_size("cols")
    return (
        jnp.where(row > 0, 1.0, 0.0),
        jnp.where(row < nrows - 1, 1.0, 0.0),
        jnp.where(col > 0, 1.0, 0.0),
        jnp.where(col < ncols - 1, 1.0, 0.0),
    )


def neighbours():
    row, col = lax.axis_index("rows"), lax.axis_index("cols")
    nrows, ncols = lax.axis_size("rows"), lax.axis_size("cols")
    rows = (lax.rem(row + nrows - 1, nrows), row, lax.rem(row + 1, nrows))
    cols = (lax.rem(col + ncols - 1, ncols), col, lax.rem(col + 1, ncols))
    return lambda dr, dc: {"rows": rows[dr + 1], "cols": cols[dc + 1]}


def with_edges(x, left, right):
    lane = lanes((x.shape[0], 128))
    back = pltpu.roll(x, 1, 1)
    ahead = pltpu.roll(x, S - 1, 1)
    back = jnp.concatenate([jnp.where(lane == 0, left, back[:, 0:128]), back[:, 128:256]], axis=1)
    ahead = jnp.concatenate([ahead[:, 0:128], jnp.where(lane == 127, right, ahead[:, 128:256])], axis=1)
    return back, x, ahead


def store_three(ref, first_row, versions):
    for b in range(3):
        value = versions[b].astype(BF16)
        for n in range(value.shape[0] // C):
            at = (first_row + n) * 96 + b * C
            ref[at : at + C, :] = value[n * C : n * C + C, :]


def halves(x):
    high = x.astype(BF16)
    low = (x - high.astype(F32)).astype(BF16)
    return jnp.concatenate([high, low], axis=1)


def spread(b):
    cell = lax.rem(lax.broadcasted_iota(jnp.int32, (256, S), 0), 128)
    want = 31 + lax.shift_right_logical(lanes((256, S)) + (b - 1 + 4), 2)
    return jnp.where(cell == want, 1.0, 0.0).astype(BF16)


def contract(a, b):
    return lax.dot_general(a, b, (((1,), (1,)), ((), ())), preferred_element_type=F32)


def collected(total, factor):
    result = None
    for r in range(B):
        block = total[r * C : r * C + C, :]
        block = roll(jnp.concatenate([block, jnp.zeros((C, 1024 - K), F32)], axis=1), -96 * r)[:, 0:384]
        result = block if result is None else result + block
    return result * factor


def ring_plan(up, down, left, right, left_up=None, left_down=None, right_up=None, right_down=None):
    return (
        (1, 0, down, 0),
        (-1, 0, up, 1),
        (0, 1, right, 2),
        (0, -1, left, 3),
        (1, 1, right if right_down is None else right_down, 4),
        (1, -1, left if left_down is None else left_down, 5),
        (-1, 1, right if right_up is None else right_up, 6),
        (-1, -1, left if left_up is None else left_up, 7),
    )


def half(x, t):
    return x[:, t * 128 : t * 128 + 128]


def both_halves(ref, rows):
    return jnp.concatenate([ref[0, rows, :], ref[1, rows, :]], axis=1)


def main_kernel(
    factor,
    feat_hbm, cot_hbm, shift_hbm, k1_hbm, kb_hbm, k2_hbm,
    pred_hbm, out_ref,
    feat_ref, cot_ref, shift_ref, k1_ref, kb_ref, k2_ref, pred_ref,
    ft, ct, sl, sr, cl, cr, fe, xf, x3, c3, w1, w2, w2t, wb, wbt,
    act, slope, bg, pool, coarse, mu, md, el, er, gl, gr, p3, b3, pg, pf, up0, up1, up2,
    r_cot_row, r_cot_tile, r_row, r_strip, r_corner, r_gc_row, r_gc_tile, r_m, r_e,
    grad_ref, held, mine, mine_y, sums_y, sums_z,
    load_sem, store_sem, send, recv, send_a, recv_a, send_y, recv_y, send_z, recv_z, send_c, recv_c,
):
    device = neighbours()
    my_row, col, img = lax.axis_index("rows"), lax.axis_index("cols"), lax.axis_index("dp")
    nrows, ncols, ndp = lax.axis_size("rows"), lax.axis_size("cols"), lax.axis_size("dp")
    depth_z, pieces = nrows // 2, ncols // 2 * ndp
    my_x, my_high, my_low, my_z = col // 2, lax.rem(col, 2), my_row // depth_z, lax.rem(my_row, depth_z)
    me = my_x * ndp + img
    my_y = my_high * 2 + my_low

    def near(d):
        other = lax.rem(me + d, pieces)
        return other, {"cols": other // ndp * 2 + my_high, "dp": lax.rem(other, ndp)}

    def along_y(d):
        other = lax.rem(my_y + d, 4)
        return {"cols": my_x * 2 + other // 2, "rows": lax.rem(other, 2) * depth_z + my_z}

    def along_z(d):
        return {"rows": my_low * depth_z + lax.rem(my_z + d, depth_z)}

    barrier = pltpu.get_barrier_semaphore()
    greeted = [device(dr, dc) for dr in (-1, 0, 1) for dc in (-1, 0, 1) if dr or dc]
    greeted += [along_z(d) for d in range(1, depth_z)] + [along_y(d) for d in range(1, 4)]
    greeted += [near(d)[1] for d in range(1, pieces)]
    for other in greeted:
        pl.semaphore_signal(barrier, inc=1, device_id=other, device_id_type=MESH)
    loads = []
    for n, (source, target) in enumerate(
        (
            (cot_hbm, cot_ref),
            (feat_hbm, feat_ref),
            (k2_hbm, k2_ref),
            (k1_hbm, k1_ref),
            (kb_hbm, kb_ref),
            (shift_hbm, shift_ref),
        )
    ):
        loads.append(pltpu.make_async_copy(source, target, load_sem.at[n]))
        loads[-1].start()
    has_up, has_down, has_left, has_right = edge_flags()
    started = []

    def start(stage, plan, targets):
        copies = []
        for dr, dc, source, n in plan:
            copies.append(
                pltpu.make_async_remote_copy(
                    src_ref=source,
                    dst_ref=targets[n],
                    send_sem=send.at[stage, n],
                    recv_sem=recv.at[stage, n],
                    device_id=device(dr, dc),
                    device_id_type=MESH,
                )
            )
            copies[-1].start()
        started.extend(copies)
        return copies

    def arrived(copies):
        for copy in copies:
            copy.wait_recv()

    lane = lanes((C, 128))
    loads[0].wait()
    ct[...] = jnp.transpose(cot_ref[0], (1, 0, 2)).reshape(R * C, S)
    low = jnp.zeros((C, 128), BF16)
    high = jnp.zeros((C, 128), BF16)
    for r in range(R):
        at = slice(r * C, r * C + C)
        low = jnp.where(lane == r, roll(ct[at, 0:128], r), low)
        high = jnp.where(lane == r, roll(ct[at, 128:256], r - 127), high)
    cl[...] = low
    cr[...] = high
    loads[1].wait()
    ft[...] = jnp.transpose(feat_ref[0], (1, 0, 2)).reshape(R * C, S)
    for p in range(5):
        low = jnp.zeros((C, 128), BF16)
        high = jnp.zeros((C, 128), BF16)
        for g in range(7):
            r = 7 * p + g
            if r < R:
                at = slice(r * C, r * C + C)
                here = (lane >= 18 * g) & (lane < 18 * g + 17)
                low = jnp.where(here, roll(ft[at, 0:128], 18 * g), low)
                high = jnp.where(here, roll(ft[at, 128:256], 18 * g + 17), high)
        sl[p * C : p * C + C, :] = low
        sr[p * C : p * C + C, :] = high
    pl.semaphore_wait(barrier, len(greeted))
    cot_copies = start(
        0,
        ring_plan(ct.at[0:C, :], ct.at[(R - 1) * C : R * C, :], cl, cr),
        [r_cot_row.at[0], r_cot_row.at[1]] + [r_cot_tile.at[n] for n in range(6)],
    )
    feat_copies = start(
        1,
        ring_plan(
            ft.at[0 : 17 * C, :],
            ft.at[15 * C : R * C, :],
            sl,
            sr,
            sl.at[0:96, :],
            sl.at[64:160, :],
            sr.at[0:96, :],
            sr.at[64:160, :],
        ),
        [r_row.at[0], r_row.at[1], r_strip.at[0], r_strip.at[1]] + [r_corner.at[n] for n in range(4)],
    )

    for copy in loads[2:]:
        copy.wait()
    w2t[...] = banded(backward_taps(k2_ref))
    w1[...] = banded(forward_taps(k1_ref))
    wbt[...] = banded(backward_taps(kb_ref))
    wb[...] = banded(forward_taps(kb_ref))
    w2[...] = banded(forward_taps(k2_ref))
    for r in range(R):
        for t in range(2):
            at = (r + 17) * PITCH
            fe[t + 1, at : at + C, :] = ft[r * C : r * C + C, t * 128 : t * 128 + 128].astype(F32)
    cell = 32 + lax.shift_right_logical(lax.broadcasted_iota(jnp.int32, (S, 128), 0), 2)
    gather = jnp.where(cell == lanes((S, 128)), 1.0, 0.0).astype(BF16)

    def pooled(value, k, ref, scale):
        sums = jnp.dot(value, gather, preferred_element_type=F32)
        for j in range(2):
            four = sums[j * 128 : j * 128 + 128]
            four = (four[0:32] + four[32:64]) + (four[64:96] + four[96:128])
            at = (2 * k + j) * C
            ref[at : at + C, :] = (four * scale).astype(BF16)

    arrived(cot_copies)
    tiles = [r_cot_tile[n] for n in range(6)]
    left_flag, right_flag = has_left.astype(BF16), has_right.astype(BF16)
    up_flag, down_flag = has_up.astype(BF16), has_down.astype(BF16)
    for r in range(-1, R + 1):
        if r < 0:
            x = r_cot_row[0] * up_flag
            a, b, t, keep = tiles[2], tiles[3], R - 1, up_flag
        elif r == R:
            x = r_cot_row[1] * down_flag
            a, b, t, keep = tiles[4], tiles[5], 0, down_flag
        else:
            x = ct[r * C : r * C + C, :]
            a, b, t, keep = tiles[0], tiles[1], r, None
        a, b = roll(a, -t) * left_flag, roll(b, 127 - t) * right_flag
        if keep is not None:
            a, b = a * keep, b * keep
        store_three(c3, r + 1, with_edges(x, a, b))
    for k in range(R // B):
        rows = slice(k * B * C, (k + 1) * B * C)
        depth = slice(k * B * 96, k * B * 96 + K)
        value = jnp.dot(w2t[...], c3[depth, :], preferred_element_type=F32).astype(BF16)
        bg[rows, :] = value
        pooled(value, k, coarse, 1.0)
    low = jnp.zeros((C, 128), BF16)
    high = jnp.zeros((C, 128), BF16)
    for j in range(8):
        value = coarse[j * C : j * C + C, :]
        low = jnp.where(lane == j, roll(value, j - 32), low)
        high = jnp.where(lane == j, roll(value, j - 95), high)
    gl[...] = low
    gr[...] = high
    coarse_copies = start(
        2,
        ring_plan(coarse.at[0:C, :], coarse.at[7 * C : 8 * C, :], gl, gr),
        [r_gc_row.at[0], r_gc_row.at[1]] + [r_gc_tile.at[n] for n in range(6)],
    )

    arrived(feat_copies)
    for t in range(2):
        cols = slice(t * 128, t * 128 + 128)
        for r in range(17):
            rows = slice(r * C, r * C + C)
            at = r * PITCH
            fe[t + 1, at : at + C, :] = r_row[0, rows, cols].astype(F32) * has_up
            at = (r + 49) * PITCH
            fe[t + 1, at : at + C, :] = r_row[1, rows, cols].astype(F32) * has_down
    for side, mid, above, below, offset, flag in (
        (0, r_strip.at[0], r_corner.at[0], r_corner.at[2], 111, has_left),
        (3, r_strip.at[1], r_corner.at[1], r_corner.at[3], 0, has_right),
    ):
        for r in range(-17, R + 17):
            if r < 0:
                source, their, first, keep = above, r + R, 2, flag * has_up
            elif r >= R:
                source, their, first, keep = below, r - R, 0, flag * has_down
            else:
                source, their, first, keep = mid, r, 0, flag
            at = (their // 7 - first) * C
            value = source[at : at + C, :].astype(F32)
            fe[side, (r + 17) * PITCH : (r + 17) * PITCH + C, :] = roll(value, offset - 18 * (their % 7)) * keep

    long_lane = lanes((R + 2, 128))
    for c in range(C):
        row_shift, col_shift = shift_ref[0, 0, c], shift_ref[0, 1, c]
        turn = lax.rem(128 - col_shift, 128)
        turned = [
            pltpu.roll(fe[t, pl.ds((M + row_shift) * PITCH + c, R + 2, stride=PITCH), :], turn, 1)
            for t in range(4)
        ]
        before = long_lane + col_shift < 0
        after = long_lane + col_shift >= 128
        rows = pl.ds(c, R + 2, stride=PITCH)
        for t in range(2):
            xf[t, rows, :] = jnp.where(before, turned[t], jnp.where(after, turned[t + 2], turned[t + 1]))
        xf[2, rows, :] = jnp.where(
            long_lane >= 64,
            jnp.where(after, turned[1], turned[0]),
            jnp.where(before, turned[2], turned[3]),
        )
    wide = lanes((C, S))
    first_lane = jnp.where(wide == 0, has_left, 1.0)
    last_lane = jnp.where(wide == S - 1, has_right, 1.0)
    edge_lane = jnp.where(lane >= 64, has_left, has_right)
    for row in range(R + 2):
        at = slice(row * PITCH, row * PITCH + C)
        x = both_halves(xf, at)
        edge = xf[2, at, :] * edge_lane
        if row == 0 or row == R + 1:
            keep = has_up if row == 0 else has_down
            x, edge = x * keep, edge * keep
        edge = edge.astype(BF16)
        store_three(x3, row, with_edges(x.astype(BF16), roll(edge, 1), roll(edge, 127)))

    for k in range(R // B):
        rows = slice(k * B * C, (k + 1) * B * C)
        depth = slice(k * B * 96, k * B * 96 + K)
        pre = jnp.dot(w1[...], x3[depth, :], preferred_element_type=F32)
        sigma = 1.0 / (1.0 + jnp.exp(-pre))
        value = (pre * sigma).astype(BF16)
        act[rows, :] = value
        slope[rows, :] = sigma * (1.0 + pre * (1.0 - sigma))
        pooled(value, k, pool, 1.0 / 16.0)
    mu[0:32, :] = act[0:32, 0:128]
    mu[32:64, :] = act[0:32, 128:256]
    mu[64:128, :] = pool[0:64, :]
    md[0:32, :] = act[31 * C :, 0:128]
    md[32:64, :] = act[31 * C :, 128:256]
    md[64:128, :] = pool[192:256, :]
    low = jnp.zeros((C, 128), BF16)
    high = jnp.zeros((C, 128), BF16)
    for j in range(8):
        for v in range(4):
            at = (4 * j + v) * C
            t = 8 * j + v
            low = jnp.where(lane == t, roll(act[at : at + C, 0:128], t), low)
            high = jnp.where(lane == t, roll(act[at : at + C, 128:256], t - 127), high)
        t = 8 * j + 4
        two = (lane == t) | (lane == t + 1)
        value = pool[j * C : j * C + C, :]
        low = jnp.where(two, roll(value, t - 32), low)
        high = jnp.where(two, roll(value, t - 94), high)
    el[...] = low
    er[...] = high
    edge_copies = start(
        3, ring_plan(mu, md, el, er), [r_m.at[0], r_m.at[1]] + [r_e.at[n] for n in range(6)]
    )

    def cells(width, centre, tile_refs, lane_of):
        left_tiles = [2] * 2 + [0] * 8 + [4] * 2
        for row in range(-width, 8 + width):
            n = left_tiles[row + 2]
            t = lane_of(row % 8)
            x = centre(row).astype(F32)
            left = roll(tile_refs[n].astype(F32), 32 - width - t)
            right = roll(tile_refs[n + 1].astype(F32), 96 - t)
            x = jnp.where((lane >= 32 - width) & (lane < 32), left * has_left, x)
            x = jnp.where((lane >= 96) & (lane < 96 + width), right * has_right, x)
            if row < 0 or row >= 8:
                x = x * (has_up if row < 0 else has_down)
            for b in range(3):
                at = (row + width) * 96 + b * C
                p3[at : at + C, :] = roll(x, 1 - b).astype(BF16)

    def coarse_row(row):
        if row < 0 or row >= 8:
            return r_gc_row[0 if row < 0 else 1]
        return coarse[row * C : row * C + C, :]

    def pooled_row(row):
        if row < 0:
            return r_m[0, 64 + (row + 2) * C : 64 + (row + 3) * C, :]
        if row >= 8:
            return r_m[1, 64 + (row - 8) * C : 64 + (row - 7) * C, :]
        return pool[row * C : row * C + C, :]

    arrived(coarse_copies)
    cells(1, coarse_row, r_gc_tile, lambda j: j)
    grad = jnp.dot(wbt[...], p3[0:K, :], preferred_element_type=F32)
    spread_mid = spread(1)
    up1[0:256, :] = jnp.dot(halves(grad), spread_mid, preferred_element_type=F32) * (1.0 / 16.0)
    for row in range(R):
        at = slice(row * C, row * C + C)
        cell_at = (row // 4) * C
        value = (bg[at, :].astype(F32) + up1[cell_at : cell_at + C, :]) * slope[at, :]
        pg[at, :] = value.astype(BF16)
    total = None
    for k in range(R // B):
        rows = slice(k * B * C, (k + 1) * B * C)
        depth = slice(k * B * 96, k * B * 96 + K)
        part = contract(pg[rows, :], x3[depth, :])
        total = part if total is None else total + part
    first = collected(total, factor)

    arrived(edge_copies)
    cells(2, pooled_row, r_e, lambda j: 8 * j + 4)
    bottle = jnp.concatenate(
        [
            jnp.dot(wb[...], p3[0:K, :], preferred_element_type=F32),
            jnp.dot(wb[...], p3[192 : 192 + K, :], preferred_element_type=F32)[6 * C :],
        ],
        axis=0,
    )
    parts = halves(bottle)
    for b, ref in enumerate((up0, up1, up2)):
        ref[...] = jnp.dot(parts, spread_mid if b == 1 else spread(b), preferred_element_type=F32)

    tiles = [r_e[n] for n in range(6)]
    for row in range(-1, R + 1):
        if row < 0:
            x = jnp.concatenate([r_m[0, 0:32, :], r_m[0, 32:64, :]], axis=1)
            low, high, t = tiles[2], tiles[3], 59
        elif row == R:
            x = jnp.concatenate([r_m[1, 0:32, :], r_m[1, 32:64, :]], axis=1)
            low, high, t = tiles[4], tiles[5], 0
        else:
            x = act[row * C : row * C + C, :]
            low, high, t = tiles[0], tiles[1], 8 * (row // 4) + row % 4
        at = ((row + 4) // 4) * C
        back, mid, ahead = with_edges(x, roll(low, -t), roll(high, 127 - t))
        back = (back.astype(F32) + up0[at : at + C, :]) * first_lane
        mid = mid.astype(F32) + up1[at : at + C, :]
        ahead = (ahead.astype(F32) + up2[at : at + C, :]) * last_lane
        if row < 0 or row == R:
            keep = has_up if row < 0 else has_down
            back, mid, ahead = back * keep, mid * keep, ahead * keep
        store_three(b3, row + 1, (back, mid, ahead))

    total = None
    for k in range(R // B):
        rows = slice(k * B * C, (k + 1) * B * C)
        depth = slice(k * B * 96, k * B * 96 + K)
        part = contract(ct[rows, :], b3[depth, :])
        total = part if total is None else total + part
    second = collected(total, factor)
    both = jnp.concatenate([half(x, t) for t in range(3) for x in (first, second)], axis=0)
    height = grad_ref.shape[1]
    for n in range(pieces):
        grad_ref[n] = both[n * height : (n + 1) * height, :]

    def send_to(device_id, source, target, send_sem, recv_sem):
        copy = pltpu.make_async_remote_copy(
            src_ref=source,
            dst_ref=target,
            send_sem=send_sem,
            recv_sem=recv_sem,
            device_id=device_id,
            device_id_type=MESH,
        )
        copy.start()
        started.append(copy)
        return copy

    copies = []
    for d in range(1, pieces):
        other, device_id = near(d)
        copies.append(send_to(device_id, grad_ref.at[other], held.at[d], send_a.at[d], recv_a.at[d]))
    for k in range(R // B):
        rows = slice(k * B * C, (k + 1) * B * C)
        depth = slice(k * B * 96, k * B * 96 + K)
        pf[rows, :] = jnp.dot(w2[...], b3[depth, :], preferred_element_type=F32).astype(BF16)
    arrived(copies)
    total = grad_ref[me]
    for d in range(1, pieces):
        total = total + held[d]
    mine[...] = total
    sums_y[my_y] = total
    copies = []
    for d in range(1, 4):
        copies.append(send_to(along_y(d), mine, sums_y.at[my_y], send_y.at[d], recv_y.at[d]))
    pred_ref[0] = jnp.transpose(pf[...].reshape(R, C, S), (1, 0, 2))
    store = pltpu.make_async_copy(pred_ref, pred_hbm, store_sem)
    store.start()
    arrived(copies)
    total = (sums_y[0] + sums_y[1]) + (sums_y[2] + sums_y[3])
    mine_y[...] = total
    sums_z[my_z] = total
    copies = []
    for d in range(1, depth_z):
        copies.append(send_to(along_z(d), mine_y, sums_z.at[my_z], send_z.at[d], recv_z.at[d]))
    arrived(copies)
    total = sums_z[0]
    for n in range(1, depth_z):
        total = total + sums_z[n]
    out_ref[me] = total
    copies = []
    for d in range(1, pieces):
        copies.append(send_to(near(d)[1], out_ref.at[me], out_ref.at[me], send_c.at[d], recv_c.at[d]))
    arrived(copies)
    store.wait()
    for copy in started:
        copy.wait_send()


def vmem(n):
    return [pl.BlockSpec(memory_space=pltpu.VMEM)] * n


def main(factor, pieces, features, cotangent, shifts, k1, kb, k2):
    def f(*shape):
        return pltpu.VMEM(shape, F32)

    def h(*shape):
        return pltpu.VMEM(shape, BF16)

    height, nrows = 192 // pieces, lax.axis_size("rows")
    depth_z = nrows // 2
    scratch = [h(1, C, R, S), h(1, C, R, S), pltpu.SMEM((1, 2, C), jnp.int32)]
    scratch += [h(9, C, C)] * 3 + [h(1, C, R, S)]
    scratch += [h(R * C, S), h(R * C, S)]
    scratch += [h(160, 128), h(160, 128), h(C, 128), h(C, 128)]
    scratch += [f(4, 72 * PITCH, 128), f(3, (R + 8) * PITCH, 128)]
    scratch += [h((R + 2) * 96, S), h((R + 2) * 96, S)] + [h(B * C, K)] * 5
    scratch += [h(R * C, S), f(R * C, S), h(R * C, S), h(256, 128), h(256, 128)]
    scratch += [h(128, 128), h(128, 128)] + [h(C, 128)] * 4
    scratch += [h(12 * 96, 128), h((R + 2) * 96, S), h(R * C, S), h(R * C, S)]
    scratch += [f(10 * C, S)] * 3
    scratch += [h(2, C, S), h(6, C, 128), h(2, 17 * C, S), h(2, 160, 128), h(4, 96, 128)]
    scratch += [h(2, C, 128), h(6, C, 128), h(2, 128, 128), h(6, C, 128)]
    scratch += [f(pieces, height, 128), f(pieces, height, 128), f(height, 128), f(height, 128)]
    scratch += [f(4, height, 128), f(depth_z, height, 128), pltpu.SemaphoreType.DMA((6,)), pltpu.SemaphoreType.DMA]
    scratch += [pltpu.SemaphoreType.DMA((4, 8)), pltpu.SemaphoreType.DMA((4, 8))]
    scratch += [pltpu.SemaphoreType.DMA((n,)) for n in (pieces, pieces, 4, 4, depth_z, depth_z, pieces, pieces)]
    hbm = pl.BlockSpec(memory_space=pl.ANY)
    return pl.pallas_call(
        functools.partial(main_kernel, factor),
        out_shape=(
            jax.ShapeDtypeStruct((1, C, R, S), BF16),
            jax.ShapeDtypeStruct((pieces, 192 // pieces, 128), F32),
        ),
        in_specs=[hbm] * 6,
        out_specs=(hbm, vmem(1)[0]),
        scratch_shapes=scratch,
        compiler_params=pltpu.CompilerParams(collective_id=0, has_side_effects=True),
        name="main",
    )(features, cotangent, shifts, k1, kb, k2)


def finish_kernel(pred_ref, sums_ref, out_ref, first_ref, second_ref, held, sem_in, sem_out):
    parts = 4
    size = C // parts
    loads, stores = [], []
    for n in range(parts):
        at = slice(n * size, n * size + size)
        loads.append(pltpu.make_async_copy(pred_ref.at[0, at], held.at[at], sem_in.at[n]))
        stores.append(pltpu.make_async_copy(held.at[at], out_ref.at[0, at], sem_out.at[n]))
        loads[n].start()
    for n in range(parts):
        loads[n].wait()
        stores[n].start()
    whole = jnp.concatenate([sums_ref[n] for n in range(sums_ref.shape[0])], axis=0)
    for t in range(9):
        for n, ref in enumerate((first_ref, second_ref)):
            at = (t // 4) * 64 + n * C
            ref[t] = roll(whole[at : at + C, :], -32 * (t % 4))[:, 0:C]
    for n in range(parts):
        stores[n].wait()


def finish(prediction, sums):
    hbm = pl.BlockSpec(memory_space=pl.ANY)
    return pl.pallas_call(
        finish_kernel,
        out_shape=(jax.ShapeDtypeStruct(prediction.shape, BF16),)
        + (jax.ShapeDtypeStruct((9, C, C), F32),) * 2,
        in_specs=[hbm] + vmem(1),
        out_specs=(hbm,) + tuple(vmem(2)),
        scratch_shapes=[
            pltpu.VMEM((C, R, S), BF16),
            pltpu.SemaphoreType.DMA((4,)),
            pltpu.SemaphoreType.DMA((4,)),
        ],
        name="finish",
    )(prediction, sums)


def shards(features, shifts, first_kernel, bottle_kernel, second_kernel, cotangent):
    nrows, ncols, ndp = lax.axis_size("rows"), lax.axis_size("cols"), lax.axis_size("dp")
    assert features.shape == (1, C, R, S)
    factor = 1.0 / math.sqrt(ndp * nrows * R * ncols * S)
    prediction, grads = main(
        factor, ncols // 2 * ndp, features, cotangent, shifts.transpose(0, 2, 1), first_kernel, bottle_kernel, second_kernel
    )
    return finish(prediction, grads)


def solution(mesh):
    placed = (
        P("dp", None, "rows", "cols"),
        P("dp", None, None),
        P(),
        P(),
        P(),
        P("dp", None, "rows", "cols"),
    )
    return jax.shard_map(
        shards,
        mesh=mesh,
        in_specs=placed,
        out_specs=(P("dp", None, "rows", "cols"), P(), P()),
        check_vma=False,
    )
```

```python
import functools
import math

import jax
import jax.numpy as jnp
from jax import lax
from jax.experimental import pallas as pl
from jax.experimental.pallas import tpu as pltpu
from jax.sharding import PartitionSpec as P

C = 32
R = 32
S = 256
M = 16
B = 8
K = (B + 2) * 3 * C
PITCH = C + 1
F32 = jnp.float32
BF16 = jnp.bfloat16
MESH = pl.DeviceIdType.MESH


def lanes(shape):
    return lax.broadcasted_iota(jnp.int32, shape, len(shape) - 1)


def roll(x, amount):
    size = x.shape[1]
    amount = amount % size
    return x if amount == 0 else pltpu.roll(x, amount, 1)


def banded(taps):
    wide = jnp.concatenate([taps, jnp.zeros((C, 1024 - 9 * C), F32)], axis=1)
    return jnp.concatenate([roll(wide, 96 * r) for r in range(B)], axis=0)[:, :K].astype(BF16)


def forward_taps(ref):
    return jnp.concatenate([ref[t].astype(F32) for t in range(9)], axis=1)


def backward_taps(ref):
    return jnp.concatenate([ref[8 - t].astype(F32) for t in range(9)], axis=0).T


def edge_flags():
    row, col = lax.axis_index("rows"), lax.axis_index("cols")
    nrows, ncols = lax.axis_size("rows"), lax.axis_size("cols")
    return (
        jnp.where(row > 0, 1.0, 0.0),
        jnp.where(row < nrows - 1, 1.0, 0.0),
        jnp.where(col > 0, 1.0, 0.0),
        jnp.where(col < ncols - 1, 1.0, 0.0),
    )


def neighbours():
    row, col = lax.axis_index("rows"), lax.axis_index("cols")
    nrows, ncols = lax.axis_size("rows"), lax.axis_size("cols")
    rows = (lax.rem(row + nrows - 1, nrows), row, lax.rem(row + 1, nrows))
    cols = (lax.rem(col + ncols - 1, ncols), col, lax.rem(col + 1, ncols))
    return lambda dr, dc: {"rows": rows[dr + 1], "cols": cols[dc + 1]}


def with_edges(x, left, right):
    lane = lanes((x.shape[0], 128))
    back = pltpu.roll(x, 1, 1)
    ahead = pltpu.roll(x, S - 1, 1)
    back = jnp.concatenate([jnp.where(lane == 0, left, back[:, 0:128]), back[:, 128:256]], axis=1)
    ahead = jnp.concatenate([ahead[:, 0:128], jnp.where(lane == 127, right, ahead[:, 128:256])], axis=1)
    return back, x, ahead


def store_three(ref, first_row, versions):
    for b in range(3):
        value = versions[b].astype(BF16)
        for n in range(value.shape[0] // C):
            at = (first_row + n) * 96 + b * C
            ref[at : at + C, :] = value[n * C : n * C + C, :]


def halves(x):
    high = x.astype(BF16)
    low = (x - high.astype(F32)).astype(BF16)
    return jnp.concatenate([high, low], axis=1)


def spread(b):
    cell = lax.rem(lax.broadcasted_iota(jnp.int32, (256, S), 0), 128)
    want = 31 + lax.shift_right_logical(lanes((256, S)) + (b - 1 + 4), 2)
    return jnp.where(cell == want, 1.0, 0.0).astype(BF16)


def contract(a, b):
    return lax.dot_general(a, b, (((1,), (1,)), ((), ())), preferred_element_type=F32)


def collected(total, factor):
    result = None
    for r in range(B):
        block = total[r * C : r * C + C, :]
        block = roll(jnp.concatenate([block, jnp.zeros((C, 1024 - K), F32)], axis=1), -96 * r)[:, 0:384]
        result = block if result is None else result + block
    return result * factor


def ring_plan(up, down, left, right, left_up=None, left_down=None, right_up=None, right_down=None):
    return (
        (1, 1, right if right_down is None else right_down, 4),
        (1, -1, left if left_down is None else left_down, 5),
        (-1, 1, right if right_up is None else right_up, 6),
        (-1, -1, left if left_up is None else left_up, 7),
        (0, 1, right, 2),
        (0, -1, left, 3),
        (1, 0, down, 0),
        (-1, 0, up, 1),
    )


def half(x, t):
    return x[:, t * 128 : t * 128 + 128]


def both_halves(ref, rows):
    return jnp.concatenate([ref[0, rows, :], ref[1, rows, :]], axis=1)


def main_kernel(
    factor,
    feat_hbm, cot_hbm, shift_hbm, k1_hbm, kb_hbm, k2_hbm,
    pred_hbm, out_ref,
    feat_ref, cot_ref, shift_ref, k1_ref, kb_ref, k2_ref, pred_ref,
    ft, ct, sl, sr, cl, cr, fe, xf, x3, c3, w1, w2, w2t, wb, wbt,
    act, slope, bg, pool, coarse, mu, md, el, er, gl, gr, p3, b3, pg, pf, up0, up1, up2,
    r_cot_row, r_cot_tile, r_row, r_strip, r_corner, r_gc_row, r_gc_tile, r_m, r_e,
    grad_ref, held, mine, mine_y, sums_y, sums_z,
    load_sem, store_sem, send, recv, send_a, recv_a, send_y, recv_y, send_z, recv_z, send_c, recv_c,
):
    device = neighbours()
    my_row, col, img = lax.axis_index("rows"), lax.axis_index("cols"), lax.axis_index("dp")
    nrows, ncols, ndp = lax.axis_size("rows"), lax.axis_size("cols"), lax.axis_size("dp")
    depth_z, pieces = nrows // 2, ncols // 2 * ndp
    my_x, my_high, my_low, my_z = col // 2, lax.rem(col, 2), my_row // depth_z, lax.rem(my_row, depth_z)
    me = my_x * ndp + img
    my_y = my_high * 2 + my_low

    def near(d):
        other = lax.rem(me + d, pieces)
        return other, {"cols": other // ndp * 2 + my_high, "dp": lax.rem(other, ndp)}

    def along_y(d):
        other = lax.rem(my_y + d, 4)
        return {"cols": my_x * 2 + other // 2, "rows": lax.rem(other, 2) * depth_z + my_z}

    def along_z(d):
        return {"rows": my_low * depth_z + lax.rem(my_z + d, depth_z)}

    barrier = pltpu.get_barrier_semaphore()
    greeted = [device(dr, dc) for dr in (-1, 0, 1) for dc in (-1, 0, 1) if dr or dc]
    greeted += [along_z(d) for d in range(1, depth_z)] + [along_y(d) for d in range(1, 4)]
    greeted += [near(d)[1] for d in range(1, pieces)]
    for other in greeted:
        pl.semaphore_signal(barrier, inc=1, device_id=other, device_id_type=MESH)
    loads = []
    for n, (source, target) in enumerate(
        (
            (cot_hbm, cot_ref),
            (feat_hbm, feat_ref),
            (k2_hbm, k2_ref),
            (k1_hbm, k1_ref),
            (kb_hbm, kb_ref),
            (shift_hbm, shift_ref),
        )
    ):
        loads.append(pltpu.make_async_copy(source, target, load_sem.at[n]))
        loads[-1].start()
    has_up, has_down, has_left, has_right = edge_flags()
    started = []

    def start(stage, plan, targets):
        copies = []
        for dr, dc, source, n in plan:
            copies.append(
                pltpu.make_async_remote_copy(
                    src_ref=source,
                    dst_ref=targets[n],
                    send_sem=send.at[stage, n],
                    recv_sem=recv.at[stage, n],
                    device_id=device(dr, dc),
                    device_id_type=MESH,
                )
            )
            copies[-1].start()
        started.extend(copies)
        return copies

    def arrived(copies):
        for copy in copies:
            copy.wait_recv()

    lane = lanes((C, 128))
    loads[0].wait()
    ct[...] = jnp.transpose(cot_ref[0], (1, 0, 2)).reshape(R * C, S)
    low = jnp.zeros((C, 128), BF16)
    high = jnp.zeros((C, 128), BF16)
    for r in range(R):
        at = slice(r * C, r * C + C)
        low = jnp.where(lane == r, roll(ct[at, 0:128], r), low)
        high = jnp.where(lane == r, roll(ct[at, 128:256], r - 127), high)
    cl[...] = low
    cr[...] = high
    loads[1].wait()
    ft[...] = jnp.transpose(feat_ref[0], (1, 0, 2)).reshape(R * C, S)
    for p in range(5):
        low = jnp.zeros((C, 128), BF16)
        high = jnp.zeros((C, 128), BF16)
        for g in range(7):
            r = 7 * p + g
            if r < R:
                at = slice(r * C, r * C + C)
                here = (lane >= 18 * g) & (lane < 18 * g + 17)
                low = jnp.where(here, roll(ft[at, 0:128], 18 * g), low)
                high = jnp.where(here, roll(ft[at, 128:256], 18 * g + 17), high)
        sl[p * C : p * C + C, :] = low
        sr[p * C : p * C + C, :] = high
    pl.semaphore_wait(barrier, len(greeted))
    cot_copies = start(
        0,
        ring_plan(ct.at[0:C, :], ct.at[(R - 1) * C : R * C, :], cl, cr),
        [r_cot_row.at[0], r_cot_row.at[1]] + [r_cot_tile.at[n] for n in range(6)],
    )
    feat_copies = start(
        1,
        ring_plan(
            ft.at[0 : 17 * C, :],
            ft.at[15 * C : R * C, :],
            sl,
            sr,
            sl.at[0:96, :],
            sl.at[64:160, :],
            sr.at[0:96, :],
            sr.at[64:160, :],
        ),
        [r_row.at[0], r_row.at[1], r_strip.at[0], r_strip.at[1]] + [r_corner.at[n] for n in range(4)],
    )

    for copy in loads[2:]:
        copy.wait()
    w2t[...] = banded(backward_taps(k2_ref))
    w1[...] = banded(forward_taps(k1_ref))
    wbt[...] = banded(backward_taps(kb_ref))
    wb[...] = banded(forward_taps(kb_ref))
    w2[...] = banded(forward_taps(k2_ref))
    for r in range(R):
        for t in range(2):
            at = (r + 17) * PITCH
            fe[t + 1, at : at + C, :] = ft[r * C : r * C + C, t * 128 : t * 128 + 128].astype(F32)
    cell = 32 + lax.shift_right_logical(lax.broadcasted_iota(jnp.int32, (S, 128), 0), 2)
    gather = jnp.where(cell == lanes((S, 128)), 1.0, 0.0).astype(BF16)

    def pooled(value, k, ref, scale):
        sums = jnp.dot(value, gather, preferred_element_type=F32)
        for j in range(2):
            four = sums[j * 128 : j * 128 + 128]
            four = (four[0:32] + four[32:64]) + (four[64:96] + four[96:128])
            at = (2 * k + j) * C
            ref[at : at + C, :] = (four * scale).astype(BF16)

    arrived(cot_copies)
    tiles = [r_cot_tile[n] for n in range(6)]
    left_flag, right_flag = has_left.astype(BF16), has_right.astype(BF16)
    up_flag, down_flag = has_up.astype(BF16), has_down.astype(BF16)
    for r in range(-1, R + 1):
        if r < 0:
            x = r_cot_row[0] * up_flag
            a, b, t, keep = tiles[2], tiles[3], R - 1, up_flag
        elif r == R:
            x = r_cot_row[1] * down_flag
            a, b, t, keep = tiles[4], tiles[5], 0, down_flag
        else:
            x = ct[r * C : r * C + C, :]
            a, b, t, keep = tiles[0], tiles[1], r, None
        a, b = roll(a, -t) * left_flag, roll(b, 127 - t) * right_flag
        if keep is not None:
            a, b = a * keep, b * keep
        store_three(c3, r + 1, with_edges(x, a, b))
    for k in range(R // B):
        rows = slice(k * B * C, (k + 1) * B * C)
        depth = slice(k * B * 96, k * B * 96 + K)
        value = jnp.dot(w2t[...], c3[depth, :], preferred_element_type=F32).astype(BF16)
        bg[rows, :] = value
        pooled(value, k, coarse, 1.0)
    low = jnp.zeros((C, 128), BF16)
    high = jnp.zeros((C, 128), BF16)
    for j in range(8):
        value = coarse[j * C : j * C + C, :]
        low = jnp.where(lane == j, roll(value, j - 32), low)
        high = jnp.where(lane == j, roll(value, j - 95), high)
    gl[...] = low
    gr[...] = high
    coarse_copies = start(
        2,
        ring_plan(coarse.at[0:C, :], coarse.at[7 * C : 8 * C, :], gl, gr),
        [r_gc_row.at[0], r_gc_row.at[1]] + [r_gc_tile.at[n] for n in range(6)],
    )

    arrived(feat_copies)
    for t in range(2):
        cols = slice(t * 128, t * 128 + 128)
        for r in range(17):
            rows = slice(r * C, r * C + C)
            at = r * PITCH
            fe[t + 1, at : at + C, :] = r_row[0, rows, cols].astype(F32) * has_up
            at = (r + 49) * PITCH
            fe[t + 1, at : at + C, :] = r_row[1, rows, cols].astype(F32) * has_down
    for side, mid, above, below, offset, flag in (
        (0, r_strip.at[0], r_corner.at[0], r_corner.at[2], 111, has_left),
        (3, r_strip.at[1], r_corner.at[1], r_corner.at[3], 0, has_right),
    ):
        for r in range(-17, R + 17):
            if r < 0:
                source, their, first, keep = above, r + R, 2, flag * has_up
            elif r >= R:
                source, their, first, keep = below, r - R, 0, flag * has_down
            else:
                source, their, first, keep = mid, r, 0, flag
            at = (their // 7 - first) * C
            value = source[at : at + C, :].astype(F32)
            fe[side, (r + 17) * PITCH : (r + 17) * PITCH + C, :] = roll(value, offset - 18 * (their % 7)) * keep

    long_lane = lanes((R + 2, 128))
    for c in range(C):
        row_shift, col_shift = shift_ref[0, 0, c], shift_ref[0, 1, c]
        turn = lax.rem(128 - col_shift, 128)
        turned = [
            pltpu.roll(fe[t, pl.ds((M + row_shift) * PITCH + c, R + 2, stride=PITCH), :], turn, 1)
            for t in range(4)
        ]
        before = long_lane + col_shift < 0
        after = long_lane + col_shift >= 128
        rows = pl.ds(c, R + 2, stride=PITCH)
        for t in range(2):
            xf[t, rows, :] = jnp.where(before, turned[t], jnp.where(after, turned[t + 2], turned[t + 1]))
        xf[2, rows, :] = jnp.where(
            long_lane >= 64,
            jnp.where(after, turned[1], turned[0]),
            jnp.where(before, turned[2], turned[3]),
        )
    wide = lanes((C, S))
    first_lane = jnp.where(wide == 0, has_left, 1.0)
    last_lane = jnp.where(wide == S - 1, has_right, 1.0)
    edge_lane = jnp.where(lane >= 64, has_left, has_right)
    for row in range(R + 2):
        at = slice(row * PITCH, row * PITCH + C)
        x = both_halves(xf, at)
        edge = xf[2, at, :] * edge_lane
        if row == 0 or row == R + 1:
            keep = has_up if row == 0 else has_down
            x, edge = x * keep, edge * keep
        edge = edge.astype(BF16)
        store_three(x3, row, with_edges(x.astype(BF16), roll(edge, 1), roll(edge, 127)))

    for k in range(R // B):
        rows = slice(k * B * C, (k + 1) * B * C)
        depth = slice(k * B * 96, k * B * 96 + K)
        pre = jnp.dot(w1[...], x3[depth, :], preferred_element_type=F32)
        sigma = 1.0 / (1.0 + jnp.exp(-pre))
        value = (pre * sigma).astype(BF16)
        act[rows, :] = value
        slope[rows, :] = sigma * (1.0 + pre * (1.0 - sigma))
        pooled(value, k, pool, 1.0 / 16.0)
    mu[0:32, :] = act[0:32, 0:128]
    mu[32:64, :] = act[0:32, 128:256]
    mu[64:128, :] = pool[0:64, :]
    md[0:32, :] = act[31 * C :, 0:128]
    md[32:64, :] = act[31 * C :, 128:256]
    md[64:128, :] = pool[192:256, :]
    low = jnp.zeros((C, 128), BF16)
    high = jnp.zeros((C, 128), BF16)
    for j in range(8):
        for v in range(4):
            at = (4 * j + v) * C
            t = 8 * j + v
            low = jnp.where(lane == t, roll(act[at : at + C, 0:128], t), low)
            high = jnp.where(lane == t, roll(act[at : at + C, 128:256], t - 127), high)
        t = 8 * j + 4
        two = (lane == t) | (lane == t + 1)
        value = pool[j * C : j * C + C, :]
        low = jnp.where(two, roll(value, t - 32), low)
        high = jnp.where(two, roll(value, t - 94), high)
    el[...] = low
    er[...] = high
    edge_copies = start(
        3, ring_plan(mu, md, el, er), [r_m.at[0], r_m.at[1]] + [r_e.at[n] for n in range(6)]
    )

    def cells(width, centre, tile_refs, lane_of):
        left_tiles = [2] * 2 + [0] * 8 + [4] * 2
        for row in range(-width, 8 + width):
            n = left_tiles[row + 2]
            t = lane_of(row % 8)
            x = centre(row).astype(F32)
            left = roll(tile_refs[n].astype(F32), 32 - width - t)
            right = roll(tile_refs[n + 1].astype(F32), 96 - t)
            x = jnp.where((lane >= 32 - width) & (lane < 32), left * has_left, x)
            x = jnp.where((lane >= 96) & (lane < 96 + width), right * has_right, x)
            if row < 0 or row >= 8:
                x = x * (has_up if row < 0 else has_down)
            for b in range(3):
                at = (row + width) * 96 + b * C
                p3[at : at + C, :] = roll(x, 1 - b).astype(BF16)

    def coarse_row(row):
        if row < 0 or row >= 8:
            return r_gc_row[0 if row < 0 else 1]
        return coarse[row * C : row * C + C, :]

    def pooled_row(row):
        if row < 0:
            return r_m[0, 64 + (row + 2) * C : 64 + (row + 3) * C, :]
        if row >= 8:
            return r_m[1, 64 + (row - 8) * C : 64 + (row - 7) * C, :]
        return pool[row * C : row * C + C, :]

    arrived(coarse_copies)
    cells(1, coarse_row, r_gc_tile, lambda j: j)
    grad = jnp.dot(wbt[...], p3[0:K, :], preferred_element_type=F32)
    spread_mid = spread(1)
    up1[0:256, :] = jnp.dot(halves(grad), spread_mid, preferred_element_type=F32) * (1.0 / 16.0)
    for row in range(R):
        at = slice(row * C, row * C + C)
        cell_at = (row // 4) * C
        value = (bg[at, :].astype(F32) + up1[cell_at : cell_at + C, :]) * slope[at, :]
        pg[at, :] = value.astype(BF16)
    total = None
    for k in range(R // B):
        rows = slice(k * B * C, (k + 1) * B * C)
        depth = slice(k * B * 96, k * B * 96 + K)
        part = contract(pg[rows, :], x3[depth, :])
        total = part if total is None else total + part
    first = collected(total, factor)

    arrived(edge_copies)
    cells(2, pooled_row, r_e, lambda j: 8 * j + 4)
    bottle = jnp.concatenate(
        [
            jnp.dot(wb[...], p3[0:K, :], preferred_element_type=F32),
            jnp.dot(wb[...], p3[192 : 192 + K, :], preferred_element_type=F32)[6 * C :],
        ],
        axis=0,
    )
    parts = halves(bottle)
    for b, ref in enumerate((up0, up1, up2)):
        ref[...] = jnp.dot(parts, spread_mid if b == 1 else spread(b), preferred_element_type=F32)

    tiles = [r_e[n] for n in range(6)]
    for row in range(-1, R + 1):
        if row < 0:
            x = jnp.concatenate([r_m[0, 0:32, :], r_m[0, 32:64, :]], axis=1)
            low, high, t = tiles[2], tiles[3], 59
        elif row == R:
            x = jnp.concatenate([r_m[1, 0:32, :], r_m[1, 32:64, :]], axis=1)
            low, high, t = tiles[4], tiles[5], 0
        else:
            x = act[row * C : row * C + C, :]
            low, high, t = tiles[0], tiles[1], 8 * (row // 4) + row % 4
        at = ((row + 4) // 4) * C
        back, mid, ahead = with_edges(x, roll(low, -t), roll(high, 127 - t))
        back = (back.astype(F32) + up0[at : at + C, :]) * first_lane
        mid = mid.astype(F32) + up1[at : at + C, :]
        ahead = (ahead.astype(F32) + up2[at : at + C, :]) * last_lane
        if row < 0 or row == R:
            keep = has_up if row < 0 else has_down
            back, mid, ahead = back * keep, mid * keep, ahead * keep
        store_three(b3, row + 1, (back, mid, ahead))

    total = None
    for k in range(R // B):
        rows = slice(k * B * C, (k + 1) * B * C)
        depth = slice(k * B * 96, k * B * 96 + K)
        part = contract(ct[rows, :], b3[depth, :])
        total = part if total is None else total + part
    second = collected(total, factor)
    both = jnp.concatenate([half(x, t) for t in range(3) for x in (first, second)], axis=0)
    height = grad_ref.shape[1]
    for n in range(pieces):
        grad_ref[n] = both[n * height : (n + 1) * height, :]

    def send_to(device_id, source, target, send_sem, recv_sem):
        copy = pltpu.make_async_remote_copy(
            src_ref=source,
            dst_ref=target,
            send_sem=send_sem,
            recv_sem=recv_sem,
            device_id=device_id,
            device_id_type=MESH,
        )
        copy.start()
        started.append(copy)
        return copy

    copies = []
    for d in range(1, pieces):
        other, device_id = near(d)
        copies.append(send_to(device_id, grad_ref.at[other], held.at[d], send_a.at[d], recv_a.at[d]))
    for k in range(R // B):
        rows = slice(k * B * C, (k + 1) * B * C)
        depth = slice(k * B * 96, k * B * 96 + K)
        pf[rows, :] = jnp.dot(w2[...], b3[depth, :], preferred_element_type=F32).astype(BF16)
    arrived(copies)
    total = grad_ref[me]
    for d in range(1, pieces):
        total = total + held[d]
    mine[...] = total
    sums_y[my_y] = total
    copies = []
    for d in range(1, 4):
        copies.append(send_to(along_y(d), mine, sums_y.at[my_y], send_y.at[d], recv_y.at[d]))
    pred_ref[0] = jnp.transpose(pf[...].reshape(R, C, S), (1, 0, 2))
    store = pltpu.make_async_copy(pred_ref, pred_hbm, store_sem)
    store.start()
    arrived(copies)
    total = (sums_y[0] + sums_y[1]) + (sums_y[2] + sums_y[3])
    mine_y[...] = total
    sums_z[my_z] = total
    copies = []
    for d in range(1, depth_z):
        copies.append(send_to(along_z(d), mine_y, sums_z.at[my_z], send_z.at[d], recv_z.at[d]))
    arrived(copies)
    total = sums_z[0]
    for n in range(1, depth_z):
        total = total + sums_z[n]
    out_ref[me] = total
    copies = []
    for d in range(1, pieces):
        copies.append(send_to(near(d)[1], out_ref.at[me], out_ref.at[me], send_c.at[d], recv_c.at[d]))
    arrived(copies)
    store.wait()
    for copy in started:
        copy.wait_send()


def vmem(n):
    return [pl.BlockSpec(memory_space=pltpu.VMEM)] * n


def main(factor, pieces, features, cotangent, shifts, k1, kb, k2):
    def f(*shape):
        return pltpu.VMEM(shape, F32)

    def h(*shape):
        return pltpu.VMEM(shape, BF16)

    height, nrows = 192 // pieces, lax.axis_size("rows")
    depth_z = nrows // 2
    scratch = [h(1, C, R, S), h(1, C, R, S), pltpu.SMEM((1, 2, C), jnp.int32)]
    scratch += [h(9, C, C)] * 3 + [h(1, C, R, S)]
    scratch += [h(R * C, S), h(R * C, S)]
    scratch += [h(160, 128), h(160, 128), h(C, 128), h(C, 128)]
    scratch += [f(4, 72 * PITCH, 128), f(3, (R + 8) * PITCH, 128)]
    scratch += [h((R + 2) * 96, S), h((R + 2) * 96, S)] + [h(B * C, K)] * 5
    scratch += [h(R * C, S), f(R * C, S), h(R * C, S), h(256, 128), h(256, 128)]
    scratch += [h(128, 128), h(128, 128)] + [h(C, 128)] * 4
    scratch += [h(12 * 96, 128), h((R + 2) * 96, S), h(R * C, S), h(R * C, S)]
    scratch += [f(10 * C, S)] * 3
    scratch += [h(2, C, S), h(6, C, 128), h(2, 17 * C, S), h(2, 160, 128), h(4, 96, 128)]
    scratch += [h(2, C, 128), h(6, C, 128), h(2, 128, 128), h(6, C, 128)]
    scratch += [f(pieces, height, 128), f(pieces, height, 128), f(height, 128), f(height, 128)]
    scratch += [f(4, height, 128), f(depth_z, height, 128), pltpu.SemaphoreType.DMA((6,)), pltpu.SemaphoreType.DMA]
    scratch += [pltpu.SemaphoreType.DMA((4, 8)), pltpu.SemaphoreType.DMA((4, 8))]
    scratch += [pltpu.SemaphoreType.DMA((n,)) for n in (pieces, pieces, 4, 4, depth_z, depth_z, pieces, pieces)]
    hbm = pl.BlockSpec(memory_space=pl.ANY)
    return pl.pallas_call(
        functools.partial(main_kernel, factor),
        out_shape=(
            jax.ShapeDtypeStruct((1, C, R, S), BF16),
            jax.ShapeDtypeStruct((pieces, 192 // pieces, 128), F32),
        ),
        in_specs=[hbm] * 6,
        out_specs=(hbm, vmem(1)[0]),
        scratch_shapes=scratch,
        compiler_params=pltpu.CompilerParams(collective_id=0, has_side_effects=True),
        name="main",
    )(features, cotangent, shifts, k1, kb, k2)


def finish_kernel(pred_ref, sums_ref, out_ref, first_ref, second_ref):
    out_ref[...] = pred_ref[...]
    whole = jnp.concatenate([sums_ref[n] for n in range(sums_ref.shape[0])], axis=0)
    for t in range(9):
        for n, ref in enumerate((first_ref, second_ref)):
            at = (t // 4) * 64 + n * C
            ref[t] = roll(whole[at : at + C, :], -32 * (t % 4))[:, 0:C]


def finish(prediction, sums):
    return pl.pallas_call(
        finish_kernel,
        out_shape=(jax.ShapeDtypeStruct(prediction.shape, BF16),)
        + (jax.ShapeDtypeStruct((9, C, C), F32),) * 2,
        in_specs=vmem(2),
        out_specs=tuple(vmem(3)),
        name="finish",
    )(prediction, sums)


def shards(features, shifts, first_kernel, bottle_kernel, second_kernel, cotangent):
    nrows, ncols, ndp = lax.axis_size("rows"), lax.axis_size("cols"), lax.axis_size("dp")
    assert features.shape == (1, C, R, S)
    factor = 1.0 / math.sqrt(ndp * nrows * R * ncols * S)
    prediction, grads = main(
        factor, ncols // 2 * ndp, features, cotangent, shifts.transpose(0, 2, 1), first_kernel, bottle_kernel, second_kernel
    )
    return finish(prediction, grads)


def solution(mesh):
    placed = (
        P("dp", None, "rows", "cols"),
        P("dp", None, None),
        P(),
        P(),
        P(),
        P("dp", None, "rows", "cols"),
    )
    return jax.shard_map(
        shards,
        mesh=mesh,
        in_specs=placed,
        out_specs=(P("dp", None, "rows", "cols"), P(), P()),
        check_vma=False,
    )
```

```python
import functools
import math

import jax
import jax.numpy as jnp
from jax import lax
from jax.experimental import pallas as pl
from jax.experimental.pallas import tpu as pltpu
from jax.sharding import PartitionSpec as P

C = 32
R = 32
S = 256
M = 16
B = 8
K = (B + 2) * 3 * C
PITCH = C + 1
F32 = jnp.float32
BF16 = jnp.bfloat16
MESH = pl.DeviceIdType.MESH


def lanes(shape):
    return lax.broadcasted_iota(jnp.int32, shape, len(shape) - 1)


def roll(x, amount):
    size = x.shape[1]
    amount = amount % size
    return x if amount == 0 else pltpu.roll(x, amount, 1)


def banded(taps):
    wide = jnp.concatenate([taps, jnp.zeros((C, 1024 - 9 * C), F32)], axis=1)
    return jnp.concatenate([roll(wide, 96 * r) for r in range(B)], axis=0)[:, :K].astype(BF16)


def forward_taps(ref):
    return jnp.concatenate([ref[t].astype(F32) for t in range(9)], axis=1)


def backward_taps(ref):
    return jnp.concatenate([ref[8 - t].astype(F32) for t in range(9)], axis=0).T


def edge_flags():
    row, col = lax.axis_index("rows"), lax.axis_index("cols")
    nrows, ncols = lax.axis_size("rows"), lax.axis_size("cols")
    return (
        jnp.where(row > 0, 1.0, 0.0),
        jnp.where(row < nrows - 1, 1.0, 0.0),
        jnp.where(col > 0, 1.0, 0.0),
        jnp.where(col < ncols - 1, 1.0, 0.0),
    )


def neighbours():
    row, col = lax.axis_index("rows"), lax.axis_index("cols")
    nrows, ncols = lax.axis_size("rows"), lax.axis_size("cols")
    rows = (lax.rem(row + nrows - 1, nrows), row, lax.rem(row + 1, nrows))
    cols = (lax.rem(col + ncols - 1, ncols), col, lax.rem(col + 1, ncols))
    return lambda dr, dc: {"rows": rows[dr + 1], "cols": cols[dc + 1]}


def with_edges(x, left, right):
    lane = lanes((x.shape[0], 128))
    back = pltpu.roll(x, 1, 1)
    ahead = pltpu.roll(x, S - 1, 1)
    back = jnp.concatenate([jnp.where(lane == 0, left, back[:, 0:128]), back[:, 128:256]], axis=1)
    ahead = jnp.concatenate([ahead[:, 0:128], jnp.where(lane == 127, right, ahead[:, 128:256])], axis=1)
    return back, x, ahead


def store_three(ref, first_row, versions):
    for b in range(3):
        value = versions[b].astype(BF16)
        for n in range(value.shape[0] // C):
            at = (first_row + n) * 96 + b * C
            ref[at : at + C, :] = value[n * C : n * C + C, :]


def halves(x):
    high = x.astype(BF16)
    low = (x - high.astype(F32)).astype(BF16)
    return jnp.concatenate([high, low], axis=1)


def spread(b):
    cell = lax.rem(lax.broadcasted_iota(jnp.int32, (256, S), 0), 128)
    want = 31 + lax.shift_right_logical(lanes((256, S)) + (b - 1 + 4), 2)
    return jnp.where(cell == want, 1.0, 0.0).astype(BF16)


def contract(a, b):
    return lax.dot_general(a, b, (((1,), (1,)), ((), ())), preferred_element_type=F32)


def collected(total, factor):
    result = None
    for r in range(B):
        block = total[r * C : r * C + C, :]
        block = roll(jnp.concatenate([block, jnp.zeros((C, 1024 - K), F32)], axis=1), -96 * r)[:, 0:384]
        result = block if result is None else result + block
    return result * factor


def ring_plan(up, down, left, right, left_up=None, left_down=None, right_up=None, right_down=None):
    return (
        (1, 1, right if right_down is None else right_down, 4),
        (1, -1, left if left_down is None else left_down, 5),
        (-1, 1, right if right_up is None else right_up, 6),
        (-1, -1, left if left_up is None else left_up, 7),
        (0, 1, right, 2),
        (0, -1, left, 3),
        (1, 0, down, 0),
        (-1, 0, up, 1),
    )


def half(x, t):
    return x[:, t * 128 : t * 128 + 128]


def both_halves(ref, rows):
    return jnp.concatenate([ref[0, rows, :], ref[1, rows, :]], axis=1)


def main_kernel(
    factor,
    feat_hbm, cot_hbm, shift_hbm, k1_hbm, kb_hbm, k2_hbm,
    pred_hbm, out_ref,
    feat_ref, cot_ref, shift_ref, k1_ref, kb_ref, k2_ref, pred_ref,
    ft, ct, sl, sr, fe, xf, x3, c3, w1, w2, w2t, wb, wbt,
    act, slope, bg, pool, coarse, mu, md, el, er, gl, gr, p3, b3, pg, pf, up0, up1, up2,
    r_cot_row, r_row, r_strip, r_corner, r_gc_row, r_gc_tile, r_m, r_e,
    grad_ref, held, mine, mine_y, sums_y, sums_z,
    load_sem, store_sem, send, recv, send_a, recv_a, send_y, recv_y, send_z, recv_z, send_c, recv_c,
):
    device = neighbours()
    my_row, col, img = lax.axis_index("rows"), lax.axis_index("cols"), lax.axis_index("dp")
    nrows, ncols, ndp = lax.axis_size("rows"), lax.axis_size("cols"), lax.axis_size("dp")
    depth_z, pieces = nrows // 2, ncols // 2 * ndp
    my_x, my_high, my_low, my_z = col // 2, lax.rem(col, 2), my_row // depth_z, lax.rem(my_row, depth_z)
    me = my_x * ndp + img
    my_y = my_high * 2 + my_low

    def near(d):
        other = lax.rem(me + d, pieces)
        return other, {"cols": other // ndp * 2 + my_high, "dp": lax.rem(other, ndp)}

    def along_y(d):
        other = lax.rem(my_y + d, 4)
        return {"cols": my_x * 2 + other // 2, "rows": lax.rem(other, 2) * depth_z + my_z}

    def along_z(d):
        return {"rows": my_low * depth_z + lax.rem(my_z + d, depth_z)}

    barrier = pltpu.get_barrier_semaphore()
    greeted = [device(dr, dc) for dr in (-1, 0, 1) for dc in (-1, 0, 1) if dr or dc]
    greeted += [along_z(d) for d in range(1, depth_z)] + [along_y(d) for d in range(1, 4)]
    greeted += [near(d)[1] for d in range(1, pieces)]
    for other in greeted:
        pl.semaphore_signal(barrier, inc=1, device_id=other, device_id_type=MESH)
    loads = []
    for n, (source, target) in enumerate(
        (
            (cot_hbm, cot_ref),
            (feat_hbm, feat_ref),
            (k2_hbm, k2_ref),
            (k1_hbm, k1_ref),
            (kb_hbm, kb_ref),
            (shift_hbm, shift_ref),
        )
    ):
        loads.append(pltpu.make_async_copy(source, target, load_sem.at[n]))
        loads[-1].start()
    has_up, has_down, has_left, has_right = edge_flags()
    started = []

    def start(stage, plan, targets):
        copies = []
        for dr, dc, source, n in plan:
            copies.append(
                pltpu.make_async_remote_copy(
                    src_ref=source,
                    dst_ref=targets[n],
                    send_sem=send.at[stage, n],
                    recv_sem=recv.at[stage, n],
                    device_id=device(dr, dc),
                    device_id_type=MESH,
                )
            )
            copies[-1].start()
        started.extend(copies)
        return copies

    def settle():
        for copy in started:
            copy.wait_send()
        started.clear()

    def arrived(copies):
        for copy in copies:
            copy.wait_recv()

    lane = lanes((C, 128))
    loads[0].wait()
    ct[...] = jnp.transpose(cot_ref[0], (1, 0, 2)).reshape(R * C, S)
    loads[1].wait()
    ft[...] = jnp.transpose(feat_ref[0], (1, 0, 2)).reshape(R * C, S)
    for p in range(5):
        low = jnp.zeros((C, 128), BF16)
        high = jnp.zeros((C, 128), BF16)
        for g in range(7):
            r = 7 * p + g
            if r < R:
                at = slice(r * C, r * C + C)
                here = (lane >= 18 * g) & (lane < 18 * g + 17)
                low = jnp.where(here, roll(ft[at, 0:128], 18 * g), low)
                high = jnp.where(here, roll(ft[at, 128:256], 18 * g + 17), high)
                spare = 18 * g + 17
                low = jnp.where(lane == spare, roll(ct[at, 0:128], spare), low)
                high = jnp.where(lane == spare, roll(ct[at, 128:256], spare - 127), high)
        sl[p * C : p * C + C, :] = low
        sr[p * C : p * C + C, :] = high
    pl.semaphore_wait(barrier, len(greeted))
    cot_copies = start(
        0,
        ring_plan(ct.at[0:C, :], ct.at[(R - 1) * C : R * C, :], None, None)[6:],
        [r_cot_row.at[0], r_cot_row.at[1]],
    )
    feat_copies = start(
        1,
        ring_plan(
            ft.at[0 : 17 * C, :],
            ft.at[15 * C : R * C, :],
            sl,
            sr,
            sl.at[0:96, :],
            sl.at[64:160, :],
            sr.at[0:96, :],
            sr.at[64:160, :],
        ),
        [r_row.at[0], r_row.at[1], r_strip.at[0], r_strip.at[1]] + [r_corner.at[n] for n in range(4)],
    )

    for copy in loads[2:]:
        copy.wait()
    w2t[...] = banded(backward_taps(k2_ref))
    w1[...] = banded(forward_taps(k1_ref))
    wbt[...] = banded(backward_taps(kb_ref))
    wb[...] = banded(forward_taps(kb_ref))
    w2[...] = banded(forward_taps(k2_ref))
    for r in range(R):
        for t in range(2):
            at = (r + 17) * PITCH
            fe[t + 1, at : at + C, :] = ft[r * C : r * C + C, t * 128 : t * 128 + 128].astype(F32)
    cell = 32 + lax.shift_right_logical(lax.broadcasted_iota(jnp.int32, (S, 128), 0), 2)
    gather = jnp.where(cell == lanes((S, 128)), 1.0, 0.0).astype(BF16)

    def pooled(value, k, ref, scale):
        sums = jnp.dot(value, gather, preferred_element_type=F32)
        for j in range(2):
            four = sums[j * 128 : j * 128 + 128]
            four = (four[0:32] + four[32:64]) + (four[64:96] + four[96:128])
            at = (2 * k + j) * C
            ref[at : at + C, :] = (four * scale).astype(BF16)

    for r in range(R):
        x = ct[r * C : r * C + C, :]
        store_three(c3, r + 1, (roll(x, 1), x, roll(x, S - 1)))

    arrived(cot_copies + feat_copies[:6])
    left_flag, right_flag = has_left.astype(BF16), has_right.astype(BF16)
    up_flag, down_flag = has_up.astype(BF16), has_down.astype(BF16)
    for r in range(-1, R + 1):
        if r < 0:
            x = r_cot_row[0] * up_flag
            a, b, t, keep = r_corner[0, 64:96, :], r_corner[1, 64:96, :], 3, up_flag
        elif r == R:
            x = r_cot_row[1] * down_flag
            a, b, t, keep = r_corner[2, 0:32, :], r_corner[3, 0:32, :], 0, down_flag
        else:
            at = (r // 7) * C
            a, b, t, keep = r_strip[0, at : at + C, :], r_strip[1, at : at + C, :], r % 7, None
        a, b = roll(a, -(18 * t + 17)) * left_flag, roll(b, 110 - 18 * t) * right_flag
        if keep is None:
            at = (r + 1) * 96
            c3[at : at + C, 0:128] = jnp.where(lane == 0, a, c3[at : at + C, 0:128])
            at += 2 * C
            c3[at : at + C, 128:256] = jnp.where(lane == 127, b, c3[at : at + C, 128:256])
        else:
            store_three(c3, r + 1, with_edges(x, a * keep, b * keep))
    for k in range(R // B):
        rows = slice(k * B * C, (k + 1) * B * C)
        depth = slice(k * B * 96, k * B * 96 + K)
        value = jnp.dot(w2t[...], c3[depth, :], preferred_element_type=F32).astype(BF16)
        bg[rows, :] = value
        pooled(value, k, coarse, 1.0)
    low = jnp.zeros((C, 128), BF16)
    high = jnp.zeros((C, 128), BF16)
    for j in range(8):
        value = coarse[j * C : j * C + C, :]
        low = jnp.where(lane == j, roll(value, j - 32), low)
        high = jnp.where(lane == j, roll(value, j - 95), high)
    gl[...] = low
    gr[...] = high
    coarse_copies = start(
        2,
        ring_plan(coarse.at[0:C, :], coarse.at[7 * C : 8 * C, :], gl, gr),
        [r_gc_row.at[0], r_gc_row.at[1]] + [r_gc_tile.at[n] for n in range(6)],
    )

    arrived(feat_copies[6:])
    for t in range(2):
        cols = slice(t * 128, t * 128 + 128)
        for r in range(17):
            rows = slice(r * C, r * C + C)
            at = r * PITCH
            fe[t + 1, at : at + C, :] = r_row[0, rows, cols].astype(F32) * has_up
            at = (r + 49) * PITCH
            fe[t + 1, at : at + C, :] = r_row[1, rows, cols].astype(F32) * has_down
    for side, mid, above, below, offset, flag in (
        (0, r_strip.at[0], r_corner.at[0], r_corner.at[2], 111, has_left),
        (3, r_strip.at[1], r_corner.at[1], r_corner.at[3], 0, has_right),
    ):
        for r in range(-17, R + 17):
            if r < 0:
                source, their, first, keep = above, r + R, 2, flag * has_up
            elif r >= R:
                source, their, first, keep = below, r - R, 0, flag * has_down
            else:
                source, their, first, keep = mid, r, 0, flag
            at = (their // 7 - first) * C
            value = source[at : at + C, :].astype(F32)
            fe[side, (r + 17) * PITCH : (r + 17) * PITCH + C, :] = roll(value, offset - 18 * (their % 7)) * keep

    long_lane = lanes((R + 2, 128))
    for c in range(C):
        row_shift, col_shift = shift_ref[0, 0, c], shift_ref[0, 1, c]
        turn = lax.rem(128 - col_shift, 128)
        turned = [
            pltpu.roll(fe[t, pl.ds((M + row_shift) * PITCH + c, R + 2, stride=PITCH), :], turn, 1)
            for t in range(4)
        ]
        before = long_lane + col_shift < 0
        after = long_lane + col_shift >= 128
        rows = pl.ds(c, R + 2, stride=PITCH)
        for t in range(2):
            xf[t, rows, :] = jnp.where(before, turned[t], jnp.where(after, turned[t + 2], turned[t + 1]))
        xf[2, rows, :] = jnp.where(
            long_lane >= 64,
            jnp.where(after, turned[1], turned[0]),
            jnp.where(before, turned[2], turned[3]),
        )
    edge_lane = jnp.where(lane >= 64, has_left, has_right)
    for row in range(R + 2):
        at = slice(row * PITCH, row * PITCH + C)
        x = both_halves(xf, at)
        edge = xf[2, at, :] * edge_lane
        if row == 0 or row == R + 1:
            keep = has_up if row == 0 else has_down
            x, edge = x * keep, edge * keep
        edge = edge.astype(BF16)
        store_three(x3, row, with_edges(x.astype(BF16), roll(edge, 1), roll(edge, 127)))

    for k in range(R // B):
        rows = slice(k * B * C, (k + 1) * B * C)
        depth = slice(k * B * 96, k * B * 96 + K)
        pre = jnp.dot(w1[...], x3[depth, :], preferred_element_type=F32)
        sigma = 1.0 / (1.0 + jnp.exp(-pre))
        value = (pre * sigma).astype(BF16)
        act[rows, :] = value
        slope[rows, :] = sigma * (1.0 + pre * (1.0 - sigma))
        pooled(value, k, pool, 1.0 / 16.0)
    mu[0:32, :] = act[0:32, 0:128]
    mu[32:64, :] = act[0:32, 128:256]
    mu[64:128, :] = pool[0:64, :]
    md[0:32, :] = act[31 * C :, 0:128]
    md[32:64, :] = act[31 * C :, 128:256]
    md[64:128, :] = pool[192:256, :]
    low = jnp.zeros((C, 128), BF16)
    high = jnp.zeros((C, 128), BF16)
    for j in range(8):
        for v in range(4):
            at = (4 * j + v) * C
            t = 8 * j + v
            low = jnp.where(lane == t, roll(act[at : at + C, 0:128], t), low)
            high = jnp.where(lane == t, roll(act[at : at + C, 128:256], t - 127), high)
        t = 8 * j + 4
        two = (lane == t) | (lane == t + 1)
        value = pool[j * C : j * C + C, :]
        low = jnp.where(two, roll(value, t - 32), low)
        high = jnp.where(two, roll(value, t - 94), high)
    el[...] = low
    er[...] = high
    edge_copies = start(
        3, ring_plan(mu, md, el, er), [r_m.at[0], r_m.at[1]] + [r_e.at[n] for n in range(6)]
    )

    def cells(width, centre, tile_refs, lane_of):
        left_tiles = [2] * 2 + [0] * 8 + [4] * 2
        for row in range(-width, 8 + width):
            n = left_tiles[row + 2]
            t = lane_of(row % 8)
            x = centre(row).astype(F32)
            left = roll(tile_refs[n].astype(F32), 32 - width - t)
            right = roll(tile_refs[n + 1].astype(F32), 96 - t)
            x = jnp.where((lane >= 32 - width) & (lane < 32), left * has_left, x)
            x = jnp.where((lane >= 96) & (lane < 96 + width), right * has_right, x)
            if row < 0 or row >= 8:
                x = x * (has_up if row < 0 else has_down)
            for b in range(3):
                at = (row + width) * 96 + b * C
                p3[at : at + C, :] = roll(x, 1 - b).astype(BF16)

    def coarse_row(row):
        if row < 0 or row >= 8:
            return r_gc_row[0 if row < 0 else 1]
        return coarse[row * C : row * C + C, :]

    def pooled_row(row):
        if row < 0:
            return r_m[0, 64 + (row + 2) * C : 64 + (row + 3) * C, :]
        if row >= 8:
            return r_m[1, 64 + (row - 8) * C : 64 + (row - 7) * C, :]
        return pool[row * C : row * C + C, :]

    arrived(coarse_copies)
    cells(1, coarse_row, r_gc_tile, lambda j: j)
    grad = jnp.dot(wbt[...], p3[0:K, :], preferred_element_type=F32)
    spread_mid = spread(1)
    up1[0:256, :] = jnp.dot(halves(grad), spread_mid, preferred_element_type=F32) * (1.0 / 16.0)
    for row in range(R):
        at = slice(row * C, row * C + C)
        cell_at = (row // 4) * C
        value = (bg[at, :].astype(F32) + up1[cell_at : cell_at + C, :]) * slope[at, :]
        pg[at, :] = value.astype(BF16)
    total = None
    for k in range(R // B):
        rows = slice(k * B * C, (k + 1) * B * C)
        depth = slice(k * B * 96, k * B * 96 + K)
        part = contract(pg[rows, :], x3[depth, :])
        total = part if total is None else total + part
    first = collected(total, factor)

    spreads = (spread(0), spread_mid, spread(2))
    first_lane = jnp.where(lanes((1, S)) == 0, has_left, 1.0)
    last_lane = jnp.where(lanes((1, S)) == S - 1, has_right, 1.0)
    arrived(edge_copies)
    cells(2, pooled_row, r_e, lambda j: 8 * j + 4)
    bottle = jnp.concatenate(
        [
            jnp.dot(wb[...], p3[0:K, :], preferred_element_type=F32),
            jnp.dot(wb[...], p3[192 : 192 + K, :], preferred_element_type=F32)[6 * C :],
        ],
        axis=0,
    )
    parts = halves(bottle)
    for b, ref in enumerate((up0, up1, up2)):
        value = jnp.dot(parts, spreads[b], preferred_element_type=F32)
        ref[...] = value if b == 1 else value * (first_lane if b == 0 else last_lane)

    tiles = [r_e[n] * (right_flag if n % 2 else left_flag) for n in range(6)]
    for row in range(-1, R + 1):
        if row < 0:
            x = jnp.concatenate([r_m[0, 0:32, :], r_m[0, 32:64, :]], axis=1)
            low, high, t = tiles[2], tiles[3], 59
        elif row == R:
            x = jnp.concatenate([r_m[1, 0:32, :], r_m[1, 32:64, :]], axis=1)
            low, high, t = tiles[4], tiles[5], 0
        else:
            x = act[row * C : row * C + C, :]
            low, high, t = tiles[0], tiles[1], 8 * (row // 4) + row % 4
        at = ((row + 4) // 4) * C
        back, mid, ahead = with_edges(x, roll(low, -t), roll(high, 127 - t))
        back = back.astype(F32) + up0[at : at + C, :]
        mid = mid.astype(F32) + up1[at : at + C, :]
        ahead = ahead.astype(F32) + up2[at : at + C, :]
        if row < 0 or row == R:
            keep = has_up if row < 0 else has_down
            back, mid, ahead = back * keep, mid * keep, ahead * keep
        store_three(b3, row + 1, (back, mid, ahead))

    total = None
    for k in range(R // B):
        rows = slice(k * B * C, (k + 1) * B * C)
        depth = slice(k * B * 96, k * B * 96 + K)
        part = contract(ct[rows, :], b3[depth, :])
        total = part if total is None else total + part
    second = collected(total, factor)
    both = jnp.concatenate([half(x, t) for t in range(3) for x in (first, second)], axis=0)
    height = grad_ref.shape[1]
    for n in range(pieces):
        grad_ref[n] = both[n * height : (n + 1) * height, :]

    def send_to(device_id, source, target, send_sem, recv_sem):
        copy = pltpu.make_async_remote_copy(
            src_ref=source,
            dst_ref=target,
            send_sem=send_sem,
            recv_sem=recv_sem,
            device_id=device_id,
            device_id_type=MESH,
        )
        copy.start()
        started.append(copy)
        return copy

    copies = []
    for d in range(1, pieces):
        other, device_id = near(d)
        copies.append(send_to(device_id, grad_ref.at[other], held.at[d], send_a.at[d], recv_a.at[d]))
    for k in range(R // B):
        rows = slice(k * B * C, (k + 1) * B * C)
        depth = slice(k * B * 96, k * B * 96 + K)
        pf[rows, :] = jnp.dot(w2[...], b3[depth, :], preferred_element_type=F32).astype(BF16)
    arrived(copies)
    total = grad_ref[me]
    for d in range(1, pieces):
        total = total + held[d]
    mine[...] = total
    sums_y[my_y] = total
    copies = []
    for d in range(1, 4):
        copies.append(send_to(along_y(d), mine, sums_y.at[my_y], send_y.at[d], recv_y.at[d]))
    pred_ref[0] = jnp.transpose(pf[...].reshape(R, C, S), (1, 0, 2))
    store = pltpu.make_async_copy(pred_ref, pred_hbm, store_sem)
    store.start()
    settle()
    arrived(copies)
    total = (sums_y[0] + sums_y[1]) + (sums_y[2] + sums_y[3])
    mine_y[...] = total
    sums_z[my_z] = total
    copies = []
    for d in range(1, depth_z):
        copies.append(send_to(along_z(d), mine_y, sums_z.at[my_z], send_z.at[d], recv_z.at[d]))
    store.wait()
    arrived(copies)
    total = sums_z[0]
    for n in range(1, depth_z):
        total = total + sums_z[n]
    out_ref[me] = total
    copies = []
    for d in range(1, pieces):
        copies.append(send_to(near(d)[1], out_ref.at[me], out_ref.at[me], send_c.at[d], recv_c.at[d]))
    settle()
    arrived(copies)


def vmem(n):
    return [pl.BlockSpec(memory_space=pltpu.VMEM)] * n


def main(factor, pieces, features, cotangent, shifts, k1, kb, k2):
    def f(*shape):
        return pltpu.VMEM(shape, F32)

    def h(*shape):
        return pltpu.VMEM(shape, BF16)

    height, nrows = 192 // pieces, lax.axis_size("rows")
    depth_z = nrows // 2
    scratch = [h(1, C, R, S), h(1, C, R, S), pltpu.SMEM((1, 2, C), jnp.int32)]
    scratch += [h(9, C, C)] * 3 + [h(1, C, R, S)]
    scratch += [h(R * C, S), h(R * C, S)]
    scratch += [h(160, 128), h(160, 128)]
    scratch += [f(4, 72 * PITCH, 128), f(3, (R + 8) * PITCH, 128)]
    scratch += [h((R + 2) * 96, S), h((R + 2) * 96, S)] + [h(B * C, K)] * 5
    scratch += [h(R * C, S), f(R * C, S), h(R * C, S), h(256, 128), h(256, 128)]
    scratch += [h(128, 128), h(128, 128)] + [h(C, 128)] * 4
    scratch += [h(12 * 96, 128), h((R + 2) * 96, S), h(R * C, S), h(R * C, S)]
    scratch += [f(10 * C, S)] * 3
    scratch += [h(2, C, S), h(2, 17 * C, S), h(2, 160, 128), h(4, 96, 128)]
    scratch += [h(2, C, 128), h(6, C, 128), h(2, 128, 128), h(6, C, 128)]
    scratch += [f(pieces, height, 128), f(pieces, height, 128), f(height, 128), f(height, 128)]
    scratch += [f(4, height, 128), f(depth_z, height, 128), pltpu.SemaphoreType.DMA((6,)), pltpu.SemaphoreType.DMA]
    scratch += [pltpu.SemaphoreType.DMA((4, 8)), pltpu.SemaphoreType.DMA((4, 8))]
    scratch += [pltpu.SemaphoreType.DMA((n,)) for n in (pieces, pieces, 4, 4, depth_z, depth_z, pieces, pieces)]
    hbm = pl.BlockSpec(memory_space=pl.ANY)
    return pl.pallas_call(
        functools.partial(main_kernel, factor),
        out_shape=(
            jax.ShapeDtypeStruct((1, C, R, S), BF16),
            jax.ShapeDtypeStruct((pieces, 192 // pieces, 128), F32),
        ),
        in_specs=[hbm] * 6,
        out_specs=(hbm, vmem(1)[0]),
        scratch_shapes=scratch,
        compiler_params=pltpu.CompilerParams(collective_id=0, has_side_effects=True),
        name="main",
    )(features, cotangent, shifts, k1, kb, k2)


def finish_kernel(pred_ref, sums_ref, out_ref, first_ref, second_ref):
    out_ref[...] = pred_ref[...]
    whole = jnp.concatenate([sums_ref[n] for n in range(sums_ref.shape[0])], axis=0)
    for t in range(9):
        for n, ref in enumerate((first_ref, second_ref)):
            at = (t // 4) * 64 + n * C
            ref[t] = roll(whole[at : at + C, :], -32 * (t % 4))[:, 0:C]


def finish(prediction, sums):
    return pl.pallas_call(
        finish_kernel,
        out_shape=(jax.ShapeDtypeStruct(prediction.shape, BF16),)
        + (jax.ShapeDtypeStruct((9, C, C), F32),) * 2,
        in_specs=vmem(2),
        out_specs=tuple(vmem(3)),
        name="finish",
    )(prediction, sums)


def shards(features, shifts, first_kernel, bottle_kernel, second_kernel, cotangent):
    nrows, ncols, ndp = lax.axis_size("rows"), lax.axis_size("cols"), lax.axis_size("dp")
    assert features.shape == (1, C, R, S)
    factor = 1.0 / math.sqrt(ndp * nrows * R * ncols * S)
    prediction, grads = main(
        factor, ncols // 2 * ndp, features, cotangent, shifts.transpose(0, 2, 1), first_kernel, bottle_kernel, second_kernel
    )
    return finish(prediction, grads)


def solution(mesh):
    placed = (
        P("dp", None, "rows", "cols"),
        P("dp", None, None),
        P(),
        P(),
        P(),
        P("dp", None, "rows", "cols"),
    )
    return jax.shard_map(
        shards,
        mesh=mesh,
        in_specs=placed,
        out_specs=(P("dp", None, "rows", "cols"), P(), P()),
        check_vma=False,
    )
```
